32 devices in a mesh: req: 8 (over z, x), mlp: 4 (over y, core).
Axes of the slice: x: 2, y: 2, z: 4, core: 2. Of those that a mesh axis runs over, the one named last changes fastest.
Arguments:
- tokens: bfloat16 [8192, 2048], P('req', 'mlp'), may hold values from -40 to 40, as said below
- norm_gain_vector: bfloat16 [2048], replicated, may hold values from 0.099609375 to 1.8984375
- gate_weight: bfloat16 [2048, 3584], P(None, 'mlp'), may hold values from -0.125 to 0.125
- up_weight: bfloat16 [2048, 3584], P(None, 'mlp'), may hold values from -0.125 to 0.125
- down_weight: bfloat16 [3584, 2048], P('mlp'), may hold values from -0.09375 to 0.09375
- gate_up_input_maps: bfloat16 [8, 2048, 32], P('req'), may hold values from -0.125 to 0.125
- gate_up_output_maps: bfloat16 [8, 2, 16, 3584], P('req', None, None, 'mlp'), may hold values from -1.5 to 1.5
- down_input_maps: bfloat16 [8, 3584, 16], P('req', 'mlp'), may hold values from -0.09375 to 0.09375
- down_output_maps: bfloat16 [8, 16, 2048], P('req'), may hold values from -1.5 to 1.5
- lengths: int32 [8, 4], replicated, may hold values from 0 to 1024, as said below
- request_adapter_slot: int32 [8, 4], replicated, may hold values from 0 to 7
- selected: int32 [8], replicated, may hold values from 0 to 7, as said below
Outputs:
- layer_out: bfloat16 [8192, 2048], P('req', 'mlp')
The draws below stay inside these ranges and needn't reach their ends.
Inputs may be any that keep to these rules, and one draw needn't show every extreme that they name: Each row of lengths sums to a multiple of 64 from 64 to 1024; some row sums to exactly 1024 and holds all of it in one slot; all rows together sum to 4096. Slots may hold zero tokens. `selected`: 8 different adapter ids; adapter a is owned by index a // 1 of req. `tokens`: entries of order one, some rows and features larger than others.
All inputs are finite; a program needn't handle non-finite values.
Results may differ from the reference program's by a relative error of at most 0.006.
Values may be sent and summed in bfloat16 or wider, within the bound.
A program may use at most 128 MiB of HBM per device.

```python
import math
import jax
import jax.numpy as jnp
from jax import lax

MODEL_WIDTH = 2048
HIDDEN_UNITS = 3584
ADAPTER_RANK = 16
TOK_DEV = 512
REQ_DEV = 4
BLK = 64
CAP = 1024
ROWS = 8192
TOKENS = 4096
ADAPTER_TOTAL = 8
SEL = 8
N_REQ = 8
N_MLP = 4


def draw_tokens(key, part):
    key_noise, key_rows, key_cols = jax.random.split(jax.random.fold_in(key, 3), 3)
    noise_base = jax.random.truncated_normal(key_noise, -4.0, 4.0, (ROWS, MODEL_WIDTH), jnp.float32)
    spread_log = math.log(3.0)
    row_scale = jnp.exp(jax.random.uniform(key_rows, (ROWS, 1), jnp.float32, -spread_log, spread_log))
    col_scale = jnp.exp(jax.random.uniform(key_cols, (1, MODEL_WIDTH), jnp.float32, -spread_log, spread_log))
    return (noise_base * row_scale * col_scale).astype(jnp.bfloat16)


def draw_lengths(key, part):
    groups = TOKENS // TOK_DEV
    balanced = groups
    half_count = groups // 2
    key_order, key_pairs, key_cuts = jax.random.split(jax.random.fold_in(key, 7), 3)
    order = jax.random.permutation(key_order, groups)
    deltas = jax.random.randint(key_pairs, (half_count,), -(balanced - 1), balanced, dtype=jnp.int32)
    firsts = balanced + deltas
    seconds = balanced - deltas
    firsts = firsts.at[0].set(2 * balanced).at[1].set(balanced)
    seconds = seconds.at[0].set(1).at[1].set(balanced - 1)
    paired = jnp.stack([firsts, seconds], axis=1).reshape(groups)
    counts = jnp.zeros((groups,), jnp.int32).at[order].set(paired)
    totals = counts * BLK
    cuts = jax.random.randint(key_cuts, (groups, REQ_DEV - 1), 0, totals[:, None] + 1, dtype=jnp.int32)
    full_group = (totals == CAP)[:, None]
    cuts = jnp.where(full_group, totals[:, None], cuts)
    cuts = jnp.sort(cuts, axis=1)
    bounds = jnp.concatenate([jnp.zeros((groups, 1), jnp.int32), cuts, totals[:, None]], axis=1)
    return (bounds[:, 1:] - bounds[:, :-1]).astype(jnp.int32)


def draw_selected(key, part):
    key_middle, key_order = jax.random.split(jax.random.fold_in(key, 5), 2)
    middle = jax.random.permutation(key_middle, ADAPTER_TOTAL - 2).astype(jnp.int32) + 1
    ends = jnp.array([0, ADAPTER_TOTAL - 1], jnp.int32)
    picked = jnp.concatenate([ends, middle[:SEL - 2]], axis=0)
    shuffle = jax.random.permutation(key_order, SEL)
    return jnp.take(picked, shuffle, axis=0).astype(jnp.int32)


def with_ends(values, key, least, largest):
    longest = values.shape.index(max(values.shape))
    spots = []
    for shift in (0, 1):
        where = [jax.random.randint(jax.random.fold_in(key, axis), (), 0, length) for axis, length in enumerate(values.shape)]
        where[longest] = (where[longest] + shift) % values.shape[longest]
        spots.append(tuple(where))
    return values.at[spots[0]].set(least).at[spots[1]].set(largest)


def block_levels(stream_key, shape, cuts, low, high):
    factor_of = 1.0
    for dim, blocks in cuts:
        draws = jax.random.uniform(jax.random.fold_in(jax.random.fold_in(stream_key, 6), dim), (blocks,), jnp.float32, low / len(cuts), high / len(cuts))
        factor_of = factor_of * jnp.repeat(jnp.exp(draws), shape[dim] // blocks).reshape((-1,) + (1,) * (len(shape) - 1 - dim))
    return factor_of


def normal_values(rng, dims, width, most, pieces=(), held_as=jnp.bfloat16):
    values = width * jax.random.normal(rng, dims, jnp.float32)
    if pieces:
        values = values * block_levels(rng, dims, pieces, -0.22, 0.18)
    return jnp.clip(values, -most, most).astype(held_as)


def setup_inputs(seed: int = 0) -> dict:
    key_list = jax.random.split(jax.random.key(seed), 13)
    return {
        "tokens": draw_tokens(jax.random.fold_in(key_list[12], 71), 0),
        "norm_gain_vector": jnp.clip(1.0 + 0.18 * jax.random.normal(key_list[1], (MODEL_WIDTH,), jnp.float32), 0.099609375, 1.8984375).astype(jnp.bfloat16),
        "gate_weight": normal_values(key_list[2], (MODEL_WIDTH, HIDDEN_UNITS), MODEL_WIDTH ** -0.5, 0.125, ((1, 4),)),
        "up_weight": normal_values(key_list[3], (MODEL_WIDTH, HIDDEN_UNITS), MODEL_WIDTH ** -0.5, 0.125, ((1, 4),)),
        "down_weight": normal_values(key_list[4], (HIDDEN_UNITS, MODEL_WIDTH), HIDDEN_UNITS ** -0.5, 0.09375, ((0, 4),)),
        "gate_up_input_maps": normal_values(key_list[5], (ADAPTER_TOTAL, MODEL_WIDTH, 2 * ADAPTER_RANK), MODEL_WIDTH ** -0.5, 0.125, ((0, 8),)),
        "gate_up_output_maps": normal_values(key_list[6], (ADAPTER_TOTAL, 2, ADAPTER_RANK, HIDDEN_UNITS), ADAPTER_RANK ** -0.5, 1.5, ((0, 8), (3, 4))),
        "down_input_maps": normal_values(key_list[7], (ADAPTER_TOTAL, HIDDEN_UNITS, ADAPTER_RANK), HIDDEN_UNITS ** -0.5, 0.09375, ((0, 8), (1, 4))),
        "down_output_maps": normal_values(key_list[8], (ADAPTER_TOTAL, ADAPTER_RANK, MODEL_WIDTH), ADAPTER_RANK ** -0.5, 1.5, ((0, 8),)),
        "lengths": draw_lengths(jax.random.fold_in(key_list[12], 71), 0),
        "request_adapter_slot": with_ends(jax.random.randint(key_list[10], (N_REQ, REQ_DEV), 0, SEL), jax.random.fold_in(key_list[10], 1), 0, SEL - 1).astype(jnp.int32),
        "selected": draw_selected(jax.random.fold_in(key_list[12], 71), 0),
    }


EPSILON = 1e-06

def slot_table(owners, positions, lengths, request_adapter_slot, token_count):
    lens = jnp.take(lengths, owners, axis=0)
    req_ends = jnp.cumsum(lens, axis=1)
    starts = req_ends - lens
    inside = (positions[:, None] >= starts) & (positions[:, None] < req_ends)
    adapter_ids = jnp.take(request_adapter_slot, owners, axis=0)
    picked = lax.optimization_barrier(jnp.sum(jnp.where(inside, adapter_ids, 0), axis=1))
    live = jnp.any(inside, axis=1)
    onehot = (picked[:, None] == jnp.arange(token_count, dtype=jnp.int32)[None, :]) & live[:, None]
    return onehot.astype(jnp.float32)

def reference(tokens, norm_gain_vector, gate_weight, up_weight, down_weight, gate_up_input_maps, gate_up_output_maps, down_input_maps, down_output_maps, lengths, request_adapter_slot, selected):
    highest = lax.Precision.HIGHEST
    selected_input_maps = jnp.take(gate_up_input_maps, selected, axis=0).astype(jnp.float32)
    selected_output_maps = jnp.take(gate_up_output_maps, selected, axis=0).astype(jnp.float32)
    sel_da = jnp.take(down_input_maps, selected, axis=0).astype(jnp.float32)
    sel_db = jnp.take(down_output_maps, selected, axis=0).astype(jnp.float32)
    totals = lax.optimization_barrier(jnp.sum(lengths, axis=1))
    gain = norm_gain_vector.astype(jnp.float32)
    piece = HIDDEN_UNITS // N_MLP

    def per_device(item):
        device, block = item
        positions = jnp.arange(CAP, dtype=jnp.int32)
        owners = jnp.zeros((CAP,), jnp.int32) + device.astype(jnp.int32)
        onehot = slot_table(owners, positions, lengths, request_adapter_slot, SEL)
        values = block.astype(jnp.float32)
        mean_square = lax.optimization_barrier(jnp.mean(values * values, axis=1, keepdims=True))
        normed_input = (values * lax.rsqrt(mean_square + EPSILON) * gain).astype(jnp.bfloat16)
        low_rank_term = jnp.einsum('ec,mch->emh', normed_input.astype(jnp.float32), selected_input_maps, precision=highest) * onehot[:, :, None]
        low_rank_term = lax.optimization_barrier(low_rank_term.astype(jnp.bfloat16)).astype(jnp.float32)
        gate_sum = jnp.dot(normed_input, gate_weight, preferred_element_type=jnp.float32) + jnp.einsum('vca,can->vn', low_rank_term[:, :, :ADAPTER_RANK], selected_output_maps[:, 0], precision=highest)
        up_sum = jnp.dot(normed_input, up_weight, preferred_element_type=jnp.float32) + jnp.einsum('vca,can->vn', low_rank_term[:, :, ADAPTER_RANK:], selected_output_maps[:, 1], precision=highest)
        hidden = (jax.nn.silu(gate_sum) * up_sum).astype(jnp.bfloat16)
        hidden_wide = hidden.astype(jnp.float32)
        branch = jnp.zeros((CAP, MODEL_WIDTH), jnp.float32)
        for shard in range(N_MLP):
            low = shard * piece
            hidden_part = hidden[:, low:low + piece]
            down_rank = jnp.einsum('tf,sfr->tsr', hidden_wide[:, low:low + piece], sel_da[:, low:low + piece], precision=highest) * onehot[:, :, None]
            part = jnp.dot(hidden_part, down_weight[low:low + piece], preferred_element_type=jnp.float32) + jnp.einsum('tsr,srd->td', down_rank, sel_db, precision=highest)
            part = lax.optimization_barrier(part.astype(jnp.bfloat16)).astype(jnp.float32)
            branch = branch + part
        branch = lax.optimization_barrier(branch.astype(jnp.bfloat16)).astype(jnp.float32)
        row_valid = positions < totals[device]
        return jnp.where(row_valid[:, None], values + branch, values).astype(jnp.bfloat16)
    result = lax.map(per_device, (jnp.arange(N_REQ, dtype=jnp.int32), tokens.reshape(N_REQ, CAP, MODEL_WIDTH)))
    return result.reshape(ROWS, MODEL_WIDTH)
```

```python
import functools

import jax
import jax.numpy as jnp
from jax import lax
from jax.experimental import pallas as pl
from jax.experimental.pallas import tpu as pltpu
from jax.sharding import PartitionSpec as P

EPSILON = 1e-06
CHUNKS = 4
MESH = pl.DeviceIdType.MESH
NT = (((1,), (1,)), ((), ()))


def kernel(groups, owned, rank, slots, *refs):
    (
        lengths_ref, slot_ref, chosen_ref, tokens_ref, gain_ref, gate_ref, up_ref, down_ref,
        a_ref, b_ref, da_ref, db_ref, out_ref,
        gu_v, down_v, whole, normed, gu_sum, hidden, maps_ab, maps_d, sib_ab, sib_d,
        a_sel, bg_sel, bu_sel, da_sel, own_part, sib_out, sib_in, far_out, far_in,
        up_s, dn_s, line_r, cross_s, cross_r, af_s, af_r,
        ts_s, ts_r, tc_s, tc_r, tf_s, tf_r, rs_s, rs_r, rc_s, rc_r, local_sem,
    ) = refs
    r = lax.axis_index("req")
    m = lax.axis_index("mlp")
    half = lax.rem(m, 2)
    sib = m + 1 - 2 * half
    side = m // 2
    far = m + 2 - 4 * side
    diag = sib + 2 - 4 * side
    lane = lax.rem(r, 2)
    partner = r + 1 - 2 * lane
    place = r // 2
    places = groups // 2
    rows, cols = tokens_ref.shape
    rc = rows // CHUNKS
    parts = whole.shape[0]
    width = parts * cols
    hwidth = sib_ab.shape[2]
    inner = gate_ref.shape[1]
    span = slots * rank
    f32, bf16 = jnp.float32, jnp.bfloat16
    AB, D = 0, 1
    maps = (maps_ab, maps_d)
    sibs = (sib_ab, sib_d)

    def local(i, src, dst):
        return pltpu.make_async_copy(src, dst, local_sem.at[i])

    def remote(src, dst, ss, rs, axis, dev):
        return pltpu.make_async_remote_copy(
            src_ref=src,
            dst_ref=dst,
            send_sem=ss,
            recv_sem=rs,
            device_id={axis: dev},
            device_id_type=MESH,
        )

    def rows_of(k):
        return pl.ds(pl.multiple_of(k * rc, rc), rc)

    def up_copy(p, i):
        slot = maps[p].at[2 * i + lane]
        return remote(slot, slot, up_s.at[p, i], line_r.at[p, i], "req", r + 2)

    def down_copy(p, i):
        slot = maps[p].at[2 * i + lane]
        return remote(slot, slot, dn_s.at[p, i], line_r.at[p, i], "req", r - 2)

    def cross_copy(p, i, side_of):
        slot = maps[p].at[2 * i + side_of]
        return remote(slot, slot, cross_s.at[p, i], cross_r.at[p, i], "req", partner)

    def af_copy(p, g):
        return remote(
            maps[p].at[g, :, pl.ds(0, hwidth)], sibs[p].at[g], af_s.at[p, g], af_r.at[p, g], "mlp", sib
        )

    def tok_sib(k, who):
        return remote(
            tokens_ref.at[rows_of(k)], whole.at[who, rows_of(k)], ts_s.at[k], ts_r.at[k], "mlp", sib
        )

    def tok_far(k, who):
        return remote(
            tokens_ref.at[rows_of(k)], whole.at[who, rows_of(k)], tc_s.at[k], tc_r.at[k], "mlp", far
        )

    def tok_fwd(k, who):
        return remote(
            whole.at[far, rows_of(k)], whole.at[who, rows_of(k)], tf_s.at[k], tf_r.at[k], "mlp", sib
        )

    def part_sib(k):
        return remote(sib_out.at[k], sib_in.at[k], rs_s.at[k], rs_r.at[k], "mlp", sib)

    def part_far(k):
        return remote(far_out.at[k], far_in.at[k], rc_s.at[k], rc_r.at[k], "mlp", far)

    load_own = local(3, tokens_ref, whole.at[m])
    load_gate = local(0, gate_ref, gu_v.at[:, pl.ds(0, inner)])
    load_up = local(1, up_ref, gu_v.at[:, pl.ds(inner, inner)])
    load_down = local(2, down_ref, down_v.at[pl.ds(0, inner)])
    mine = pl.ds(pl.multiple_of(half * hwidth, hwidth), hwidth)
    other = pl.ds(pl.multiple_of((1 - half) * hwidth, hwidth), hwidth)
    left, right = pl.ds(0, hwidth), pl.ds(hwidth, inner)
    packs = []
    for o in range(owned):
        two, one = pl.ds(o * 2 * rank, 2 * rank), pl.ds(o * rank, rank)
        packs += [
            (a_ref.at[o, :, mine], maps_ab.at[r, two, left]),
            (b_ref.at[o], maps_ab.at[r, two, right]),
            (da_ref.at[o], maps_d.at[r, one, right]),
            (db_ref.at[o, :, mine], maps_d.at[r, one, left]),
        ]
    packs = [local(4 + i, src, dst) for i, (src, dst) in enumerate(packs)]
    for copy in packs:
        copy.start()

    barrier = pltpu.get_barrier_semaphore()

    def greet(axis, dev):
        pl.semaphore_signal(barrier, inc=1, device_id={axis: dev}, device_id_type=MESH)

    greet("mlp", sib)
    greet("mlp", far)
    greet("req", partner)
    inner_up = place < places - 1
    inner_down = place > 0

    @pl.when(inner_up)
    def _():
        greet("req", r + 2)

    @pl.when(inner_down)
    def _():
        greet("req", r - 2)

    below = (place + places - 1) // places
    above = (2 * (places - 1) - place) // places
    pl.semaphore_wait(barrier, 3 + below + above)

    def each(n, start=0):
        def deco(f):
            def body(i, carry):
                f(i)
                return carry

            lax.fori_loop(start, n, body, 0)

        return deco

    @each(CHUNKS)
    def _(k):
        tok_far(k, m).start()
        tok_sib(k, m).start()

    for copy in packs:
        copy.wait()

    def send_own(p):
        @pl.when(inner_up)
        def _():
            up_copy(p, place).start()

        @pl.when(inner_down)
        def _():
            down_copy(p, place).start()

        cross_copy(p, place, lane).start()
        af_copy(p, r).start()

    send_own(AB)
    for copy in (load_own, load_gate, load_up, load_down):
        copy.start()

    def relay(p, part):
        def body(d, carry):
            @pl.when(place - d >= 0)
            def _():
                i = place - d
                up_copy(p, i).wait_recv()

                @pl.when(inner_up)
                def _():
                    up_copy(p, i).start()

                cross_copy(p, i, lane).start()
                af_copy(p, 2 * i + lane).start()

            @pl.when(place + d < places)
            def _():
                i = place + d
                down_copy(p, i).wait_recv()

                @pl.when(inner_down)
                def _():
                    down_copy(p, i).start()

                cross_copy(p, i, lane).start()
                af_copy(p, 2 * i + lane).start()

            return carry

        first = 1 + (places - 1) * part // 3
        last = 1 + (places - 1) * (part + 1) // 3
        lax.fori_loop(first, last, body, 0)

    def crossed(p):
        @each(places)
        def _(i):
            cross_copy(p, i, 1 - lane).wait_recv()
            af_copy(p, 2 * i + 1 - lane).start()

    def gathered(p):
        @each(groups)
        def _(g):
            af_copy(p, g).wait_recv()

    def pick(q):
        chosen = chosen_ref[slot_ref[q, r]]
        if owned > 1:
            return chosen // owned, lax.rem(chosen, owned)
        return chosen, 0

    def take_ab():
        crossed_cols = ((mine, maps_ab), (other, sib_ab))
        bg_sel[...] = jnp.zeros_like(bg_sel)
        bu_sel[...] = jnp.zeros_like(bu_sel)
        for q in range(slots):
            g, o = pick(q)
            one, two = pl.ds(o * 2 * rank, rank), pl.ds(o * 2 * rank + rank, rank)
            at, at2 = pl.ds(q * rank, rank), pl.ds(span + q * rank, rank)
            for dst, part in crossed_cols:
                a_sel[at, dst] = part[g, one, 0:hwidth]
                a_sel[at2, dst] = part[g, two, 0:hwidth]
            bg_sel[at, :] = maps_ab[g, one, hwidth : hwidth + inner]
            bu_sel[at2, :] = maps_ab[g, two, hwidth : hwidth + inner]

    def take_d():
        for q in range(slots):
            g, o = pick(q)
            one = pl.ds(o * rank, rank)
            at, at2 = pl.ds(q * rank, rank), pl.ds(span + q * rank, rank)
            for dst, part in ((mine, maps_d), (other, sib_d)):
                db = part[g, one, 0:hwidth]
                down_v[pl.ds(inner + q * rank, rank), dst] = db
                down_v[pl.ds(inner + span + q * rank, rank), dst] = db
            da = maps_d[g, one, hwidth : hwidth + inner]
            da_sel[at, :] = da
            da_sel[at2, :] = da

    def live_rows(k):
        column = lax.broadcasted_iota(jnp.int32, (1, 2 * span), 1)
        column = jnp.where(column < span, column, column - span)
        low = jnp.zeros((1, 2 * span), jnp.int32)
        high = jnp.zeros((1, 2 * span), jnp.int32)
        end = 0
        for q in range(slots):
            own_q = (column >= q * rank) & (column < (q + 1) * rank)
            low = jnp.where(own_q, end, low)
            end = end + lengths_ref[q, r]
            high = jnp.where(own_q, end, high)
        at = lax.broadcasted_iota(jnp.int32, (rc, 2 * span), 0) + k * rc
        return (at >= low) & (at < high)

    def pass_on(k):
        tok_far(k, far).wait_recv()
        tok_fwd(k, far).start()

    def norm(k):
        here = rows_of(k)
        tok_sib(k, sib).wait_recv()
        tok_fwd(k, diag).wait_recv()
        gain_row = gain_ref[...].astype(f32).reshape(1, -1)
        squares = jnp.zeros((rc, 1), f32)
        for b in range(parts):
            x = whole[b, here, :].astype(f32)
            squares += jnp.sum(x * x, axis=1, keepdims=True)
        scale = lax.rsqrt(squares / width + EPSILON)
        for b in range(parts):
            x = whole[b, here, :].astype(f32)
            gain = gain_row[:, b * cols : (b + 1) * cols]
            normed[k, :, b * cols : (b + 1) * cols] = (x * scale * gain).astype(bf16)

    tiles = list(range(0, 2 * inner, 256))

    def base(k, first, last):
        for n0 in tiles[first:last]:
            n1 = min(n0 + 256, 2 * inner)
            gu_sum[k, :, n0:n1] = jnp.dot(normed[k], gu_v[:, n0:n1], preferred_element_type=f32)

    def gated(k):
        live = live_rows(k)
        low_rank = lax.dot_general(normed[k], a_sel[...], NT, preferred_element_type=f32)
        low_rank = jnp.where(live, low_rank, 0.0).astype(bf16)
        for n0 in range(0, inner, 256):
            n1 = min(n0 + 256, inner)
            g = gu_sum[k, :, n0:n1]
            g += jnp.dot(low_rank, bg_sel[:, n0:n1], preferred_element_type=f32)
            u = gu_sum[k, :, inner + n0 : inner + n1]
            u += jnp.dot(low_rank, bu_sel[:, n0:n1], preferred_element_type=f32)
            hidden[:, n0:n1] = (jax.nn.silu(g) * u).astype(bf16)

    def projected(k):
        live = live_rows(k)
        down_rank = lax.dot_general(hidden[:, :inner], da_sel[...], NT, preferred_element_type=f32)
        down_rank = jnp.where(live, down_rank, 0.0)
        coarse = down_rank.astype(bf16).astype(f32)
        column = lax.broadcasted_iota(jnp.int32, (rc, 2 * span), 1)
        down_rank = jnp.where(column < span, coarse, down_rank - coarse).astype(bf16)
        hidden[:, inner:] = down_rank

        def part_of(b):
            there = pl.ds(pl.multiple_of(b * cols, cols), cols)
            return jnp.dot(hidden[...], down_v[:, there], preferred_element_type=f32)

        sib_out[k, 0] = part_of(diag).astype(bf16)
        sib_out[k, 1] = part_of(sib).astype(bf16)
        part_sib(k).start()
        own_part[k, 0] = part_of(far)
        own_part[k, 1] = part_of(m)

    def reduce_far(k):
        part_sib(k).wait_recv()
        far_out[k] = (own_part[k, 0] + sib_in[k, 0].astype(f32)).astype(bf16)
        part_far(k).start()

    relay(AB, 0)
    send_own(D)
    for copy in (load_own, load_gate, load_up):
        copy.wait()

    @each(CHUNKS + 2)
    def _(j):
        has_base = j < CHUNKS
        has_rest = j >= 2

        @pl.when(j == 1)
        def _():
            relay(D, 0)
            relay(AB, 2)

        @pl.when(j == 2)
        def _():
            gathered(AB)
            take_ab()

        @pl.when(has_rest)
        def _():
            gated(j - 2)

        @pl.when(has_base)
        def _():
            pass_on(j)

        @pl.when(j == 0)
        def _():
            relay(AB, 1)

        @pl.when(j == 2)
        def _():
            crossed(D)
            gathered(D)
            load_down.wait()
            take_d()

        @pl.when(has_rest)
        def _():
            projected(j - 2)

        @pl.when(has_base)
        def _():
            norm(j)
            base(j, 0, 3)

        @pl.when(has_rest)
        def _():
            reduce_far(j - 2)

        @pl.when(j == 1)
        def _():
            relay(D, 1)
            crossed(AB)

        @pl.when(has_base)
        def _():
            base(j, 3, len(tiles))

        @pl.when(j == 1)
        def _():
            relay(D, 2)

    total = 0
    for q in range(slots):
        total = total + lengths_ref[q, r]

    @each(CHUNKS)
    def _(k):
        here = rows_of(k)
        part_far(k).wait_recv()
        branch = own_part[k, 1] + sib_in[k, 1].astype(f32) + far_in[k].astype(f32)
        branch = branch.astype(bf16).astype(f32)
        at = lax.broadcasted_iota(jnp.int32, (rc, cols), 0) + k * rc
        x = whole[m, here, :].astype(f32)
        out_ref[here, :] = jnp.where(at < total, x + branch, x).astype(out_ref.dtype)

    @each(CHUNKS)
    def _(k):
        tok_far(k, m).wait_send()
        tok_sib(k, m).wait_send()
        tok_fwd(k, far).wait_send()
        part_sib(k).wait_send()
        part_far(k).wait_send()

    for p in (AB, D):

        @each(places)
        def _(i):
            cross_copy(p, i, lane).wait_send()

            @pl.when(inner_up & (i <= place))
            def _():
                up_copy(p, i).wait_send()

            @pl.when(inner_down & (i >= place))
            def _():
                down_copy(p, i).wait_send()

        @each(groups)
        def _(g):
            af_copy(p, g).wait_send()


def on_device(
    tokens,
    norm_gain_vector,
    gate_weight,
    up_weight,
    down_weight,
    gate_up_input_maps,
    gate_up_output_maps,
    down_input_maps,
    down_output_maps,
    lengths,
    request_adapter_slot,
    selected,
):
    groups = lax.axis_size("req")
    parts = lax.axis_size("mlp")
    rows, cols = tokens.shape
    owned, rank, width = down_output_maps.shape
    inner = gate_weight.shape[1]
    slots = lengths.shape[1]
    span = slots * rank
    hwidth = width // 2
    bf16, f32 = jnp.bfloat16, jnp.float32

    rc = rows // CHUNKS
    vm, sm, hbm = (
        pl.BlockSpec(memory_space=s) for s in (pltpu.VMEM, pltpu.SMEM, pl.ANY)
    )
    dma = pltpu.SemaphoreType.DMA
    return pl.pallas_call(
        functools.partial(kernel, groups, owned, rank, slots),
        out_shape=jax.ShapeDtypeStruct((rows, cols), tokens.dtype),
        in_specs=[sm, sm, sm, hbm, vm] + [hbm] * 7,
        out_specs=vm,
        scratch_shapes=[
            pltpu.VMEM((width, 2 * inner), bf16),
            pltpu.VMEM((inner + 2 * span, width), bf16),
            pltpu.VMEM((parts, rows, cols), bf16),
            pltpu.VMEM((CHUNKS, rc, width), bf16),
            pltpu.VMEM((CHUNKS, rc, 2 * inner), f32),
            pltpu.VMEM((rc, inner + 2 * span), bf16),
            pltpu.VMEM((groups, owned * 2 * rank, hwidth + inner), bf16),
            pltpu.VMEM((groups, owned * rank, hwidth + inner), bf16),
            pltpu.VMEM((groups, owned * 2 * rank, hwidth), bf16),
            pltpu.VMEM((groups, owned * rank, hwidth), bf16),
            pltpu.VMEM((2 * span, width), bf16),
            pltpu.VMEM((2 * span, inner), bf16),
            pltpu.VMEM((2 * span, inner), bf16),
            pltpu.VMEM((2 * span, inner), bf16),
            pltpu.VMEM((CHUNKS, 2, rc, cols), f32),
            pltpu.VMEM((CHUNKS, 2, rc, cols), bf16),
            pltpu.VMEM((CHUNKS, 2, rc, cols), bf16),
            pltpu.VMEM((CHUNKS, rc, cols), bf16),
            pltpu.VMEM((CHUNKS, rc, cols), bf16),
        ]
        + [dma((2, groups // 2)) for _ in range(5)]
        + [dma((2, groups)) for _ in range(2)]
        + [dma((CHUNKS,)) for _ in range(10)]
        + [dma((4 + 4 * owned,))],
        compiler_params=pltpu.CompilerParams(
            collective_id=0, has_side_effects=True, vmem_limit_bytes=60 * 1024 * 1024
        ),
    )(
        lengths.T,
        request_adapter_slot.T,
        selected,
        tokens,
        norm_gain_vector,
        gate_weight,
        up_weight,
        down_weight,
        jnp.swapaxes(gate_up_input_maps, 1, 2),
        gate_up_output_maps.reshape(owned, 2 * rank, inner),
        jnp.swapaxes(down_input_maps, 1, 2),
        down_output_maps,
    )


def solution(mesh):
    in_specs = (
        P("req", "mlp"),
        P(),
        P(None, "mlp"),
        P(None, "mlp"),
        P("mlp", None),
        P("req", None, None),
        P("req", None, None, "mlp"),
        P("req", "mlp", None),
        P("req", None, None),
        P(),
        P(),
        P(),
    )
    return jax.shard_map(
        on_device, mesh=mesh, in_specs=in_specs, out_specs=P("req", "mlp"), check_vma=False
    )
```

```python
import functools
import math

import jax
import jax.numpy as jnp
from jax import lax
from jax.experimental import pallas as pl
from jax.experimental.pallas import tpu as pltpu
from jax.sharding import PartitionSpec as P

EPSILON = 1e-06
CHUNKS = 4
MESH = pl.DeviceIdType.MESH
NT = (((1,), (1,)), ((), ()))


def kernel(groups, owned, rank, slots, *refs):
    (
        lengths_hbm, slot_hbm, chosen_hbm, tokens_ref, gain_ref, gate_ref, up_ref, down_ref,
        a_ref, b_ref, da_ref, db_ref, out_ref,
        lengths_ref, slot_ref, chosen_ref, gu_v, down_v, whole, normed, gu_sum, hidden, maps_ab, maps_d, sib_ab, sib_d,
        a_sel, bg_sel, bu_sel, da_sel, own_part, sib_out, sib_in, far_out, far_in,
        up_s, dn_s, line_r, cross_s, cross_r, af_s, af_r,
        ts_s, ts_r, tc_s, tc_r, tf_s, tf_r, rs_s, rs_r, rc_s, rc_r, local_sem,
    ) = refs
    r = lax.axis_index("req")
    m = lax.axis_index("mlp")
    half = lax.rem(m, 2)
    sib = m + 1 - 2 * half
    side = m // 2
    far = m + 2 - 4 * side
    diag = sib + 2 - 4 * side
    lane = lax.rem(r, 2)
    partner = r + 1 - 2 * lane
    place = r // 2
    places = groups // 2
    rows, cols = tokens_ref.shape
    rc = rows // CHUNKS
    parts = whole.shape[0]
    width = parts * cols
    hwidth = sib_ab.shape[2]
    inner = gate_ref.shape[1]
    span = slots * rank
    f32, bf16 = jnp.float32, jnp.bfloat16
    AB, D = 0, 1
    maps = (maps_ab, maps_d)
    sibs = (sib_ab, sib_d)

    def local(i, src, dst):
        return pltpu.make_async_copy(src, dst, local_sem.at[i])

    def remote(src, dst, ss, rs, axis, dev):
        return pltpu.make_async_remote_copy(
            src_ref=src,
            dst_ref=dst,
            send_sem=ss,
            recv_sem=rs,
            device_id={axis: dev},
            device_id_type=MESH,
        )

    def rows_of(k):
        return pl.ds(pl.multiple_of(k * rc, rc), rc)

    def up_copy(p, i):
        slot = maps[p].at[2 * i + lane]
        return remote(slot, slot, up_s.at[p, i], line_r.at[p, i], "req", r + 2)

    def down_copy(p, i):
        slot = maps[p].at[2 * i + lane]
        return remote(slot, slot, dn_s.at[p, i], line_r.at[p, i], "req", r - 2)

    def cross_copy(p, i, side_of):
        slot = maps[p].at[2 * i + side_of]
        return remote(slot, slot, cross_s.at[p, i], cross_r.at[p, i], "req", partner)

    def af_copy(p, g):
        return remote(
            maps[p].at[g, :, pl.ds(0, hwidth)], sibs[p].at[g], af_s.at[p, g], af_r.at[p, g], "mlp", sib
        )

    def tok_sib(k, who):
        return remote(
            tokens_ref.at[rows_of(k)], whole.at[who, rows_of(k)], ts_s.at[k], ts_r.at[k], "mlp", sib
        )

    def tok_far(k, who):
        return remote(
            tokens_ref.at[rows_of(k)], whole.at[who, rows_of(k)], tc_s.at[k], tc_r.at[k], "mlp", far
        )

    def tok_fwd(k, who):
        return remote(
            whole.at[far, rows_of(k)], whole.at[who, rows_of(k)], tf_s.at[k], tf_r.at[k], "mlp", sib
        )

    def part_sib(k):
        return remote(sib_out.at[k], sib_in.at[k], rs_s.at[k], rs_r.at[k], "mlp", sib)

    def part_far(k):
        return remote(far_out.at[k], far_in.at[k], rc_s.at[k], rc_r.at[k], "mlp", far)

    tables = [
        local(4, lengths_hbm, lengths_ref),
        local(5, slot_hbm, slot_ref),
        local(6, chosen_hbm, chosen_ref),
    ]
    load_own = local(3, tokens_ref, whole.at[m])
    load_gate = local(0, gate_ref, gu_v.at[:, pl.ds(0, inner)])
    load_up = local(1, up_ref, gu_v.at[:, pl.ds(inner, inner)])
    load_down = local(2, down_ref, down_v.at[pl.ds(0, inner)])
    mine = pl.ds(pl.multiple_of(half * hwidth, hwidth), hwidth)
    other = pl.ds(pl.multiple_of((1 - half) * hwidth, hwidth), hwidth)
    left, right = pl.ds(0, hwidth), pl.ds(hwidth, inner)
    packs = []
    for o in range(owned):
        two, one = pl.ds(o * 2 * rank, 2 * rank), pl.ds(o * rank, rank)
        packs += [
            (a_ref.at[o, :, mine], maps_ab.at[r, two, left]),
            (b_ref.at[o], maps_ab.at[r, two, right]),
            (da_ref.at[o], maps_d.at[r, one, right]),
            (db_ref.at[o, :, mine], maps_d.at[r, one, left]),
        ]
    packs = [local(7 + i, src, dst) for i, (src, dst) in enumerate(packs)]
    for copy in packs:
        copy.start()

    barrier = pltpu.get_barrier_semaphore()

    def greet(axis, dev):
        pl.semaphore_signal(barrier, inc=1, device_id={axis: dev}, device_id_type=MESH)

    greet("mlp", sib)
    greet("mlp", far)
    greet("req", partner)
    inner_up = place < places - 1
    inner_down = place > 0

    @pl.when(inner_up)
    def _():
        greet("req", r + 2)

    @pl.when(inner_down)
    def _():
        greet("req", r - 2)

    below = (place + places - 1) // places
    above = (2 * (places - 1) - place) // places
    pl.semaphore_wait(barrier, 3 + below + above)

    def each(n, start=0):
        def deco(f):
            def body(i, carry):
                f(i)
                return carry

            lax.fori_loop(start, n, body, 0)

        return deco

    @each(CHUNKS)
    def _(k):
        tok_far(k, m).start()
        tok_sib(k, m).start()

    for copy in packs:
        copy.wait()

    def send_own(p):
        @pl.when(inner_up)
        def _():
            up_copy(p, place).start()

        @pl.when(inner_down)
        def _():
            down_copy(p, place).start()

        cross_copy(p, place, lane).start()
        af_copy(p, r).start()

    send_own(AB)
    for copy in [load_own, load_gate, load_up, load_down] + tables:
        copy.start()

    def relay(p, part):
        def body(d, carry):
            @pl.when(place - d >= 0)
            def _():
                i = place - d
                up_copy(p, i).wait_recv()

                @pl.when(inner_up)
                def _():
                    up_copy(p, i).start()

                cross_copy(p, i, lane).start()
                af_copy(p, 2 * i + lane).start()

            @pl.when(place + d < places)
            def _():
                i = place + d
                down_copy(p, i).wait_recv()

                @pl.when(inner_down)
                def _():
                    down_copy(p, i).start()

                cross_copy(p, i, lane).start()
                af_copy(p, 2 * i + lane).start()

            return carry

        first = 1 + (places - 1) * part // 3
        last = 1 + (places - 1) * (part + 1) // 3
        lax.fori_loop(first, last, body, 0)

    def crossed(p):
        @each(places)
        def _(i):
            cross_copy(p, i, 1 - lane).wait_recv()
            af_copy(p, 2 * i + 1 - lane).start()

    def gathered(p):
        @each(groups)
        def _(g):
            af_copy(p, g).wait_recv()

    def pick(q):
        chosen = chosen_ref[slot_ref[q, r]]
        if owned > 1:
            return chosen // owned, lax.rem(chosen, owned)
        return chosen, 0

    def take_ab():
        crossed_cols = ((mine, maps_ab), (other, sib_ab))
        bg_sel[...] = jnp.zeros_like(bg_sel)
        bu_sel[...] = jnp.zeros_like(bu_sel)
        for q in range(slots):
            g, o = pick(q)
            one, two = pl.ds(o * 2 * rank, rank), pl.ds(o * 2 * rank + rank, rank)
            at, at2 = pl.ds(q * rank, rank), pl.ds(span + q * rank, rank)
            for dst, part in crossed_cols:
                a_sel[at, dst] = part[g, one, 0:hwidth]
                a_sel[at2, dst] = part[g, two, 0:hwidth]
            bg_sel[at, :] = maps_ab[g, one, hwidth : hwidth + inner]
            bu_sel[at2, :] = maps_ab[g, two, hwidth : hwidth + inner]

    def take_d():
        for q in range(slots):
            g, o = pick(q)
            one = pl.ds(o * rank, rank)
            at, at2 = pl.ds(q * rank, rank), pl.ds(span + q * rank, rank)
            for dst, part in ((mine, maps_d), (other, sib_d)):
                db = part[g, one, 0:hwidth]
                down_v[pl.ds(inner + q * rank, rank), dst] = db
                down_v[pl.ds(inner + span + q * rank, rank), dst] = db
            da = maps_d[g, one, hwidth : hwidth + inner]
            da_sel[at, :] = da
            da_sel[at2, :] = da

    def live_rows(k):
        column = lax.broadcasted_iota(jnp.int32, (1, 2 * span), 1)
        column = jnp.where(column < span, column, column - span)
        low = jnp.zeros((1, 2 * span), jnp.int32)
        high = jnp.zeros((1, 2 * span), jnp.int32)
        end = 0
        for q in range(slots):
            own_q = (column >= q * rank) & (column < (q + 1) * rank)
            low = jnp.where(own_q, end, low)
            end = end + lengths_ref[q, r]
            high = jnp.where(own_q, end, high)
        at = lax.broadcasted_iota(jnp.int32, (rc, 2 * span), 0) + k * rc
        return (at >= low) & (at < high)

    def pass_on(k):
        tok_far(k, far).wait_recv()
        tok_fwd(k, far).start()

    def norm(k):
        here = rows_of(k)
        tok_sib(k, sib).wait_recv()
        tok_fwd(k, diag).wait_recv()
        gain_row = gain_ref[...].astype(f32).reshape(1, -1)
        squares = jnp.zeros((rc, 1), f32)
        for b in range(parts):
            x = whole[b, here, :].astype(f32)
            squares += jnp.sum(x * x, axis=1, keepdims=True)
        scale = lax.rsqrt(squares / width + EPSILON)
        for b in range(parts):
            x = whole[b, here, :].astype(f32)
            gain = gain_row[:, b * cols : (b + 1) * cols]
            normed[k, :, b * cols : (b + 1) * cols] = (x * scale * gain).astype(bf16)

    tiles = list(range(0, 2 * inner, 256))

    def base(k, first, last):
        for n0 in tiles[first:last]:
            n1 = min(n0 + 256, 2 * inner)
            gu_sum[k, :, n0:n1] = jnp.dot(normed[k], gu_v[:, n0:n1], preferred_element_type=f32)

    def gated(k):
        live = live_rows(k)
        low_rank = lax.dot_general(normed[k], a_sel[...], NT, preferred_element_type=f32)
        low_rank = jnp.where(live, low_rank, 0.0).astype(bf16)
        for n0 in range(0, inner, 256):
            n1 = min(n0 + 256, inner)
            g = gu_sum[k, :, n0:n1]
            g += jnp.dot(low_rank, bg_sel[:, n0:n1], preferred_element_type=f32)
            u = gu_sum[k, :, inner + n0 : inner + n1]
            u += jnp.dot(low_rank, bu_sel[:, n0:n1], preferred_element_type=f32)
            hidden[:, n0:n1] = (jax.nn.silu(g) * u).astype(bf16)

    def projected(k):
        live = live_rows(k)
        down_rank = lax.dot_general(hidden[:, :inner], da_sel[...], NT, preferred_element_type=f32)
        down_rank = jnp.where(live, down_rank, 0.0)
        coarse = down_rank.astype(bf16).astype(f32)
        column = lax.broadcasted_iota(jnp.int32, (rc, 2 * span), 1)
        down_rank = jnp.where(column < span, coarse, down_rank - coarse).astype(bf16)
        hidden[:, inner:] = down_rank

        def part_of(b):
            there = pl.ds(pl.multiple_of(b * cols, cols), cols)
            return jnp.dot(hidden[...], down_v[:, there], preferred_element_type=f32)

        sib_out[k, 0] = part_of(diag).astype(bf16)
        sib_out[k, 1] = part_of(sib).astype(bf16)
        part_sib(k).start()
        own_part[k, 0] = part_of(far)
        own_part[k, 1] = part_of(m)

    def reduce_far(k):
        part_sib(k).wait_recv()
        far_out[k] = (own_part[k, 0] + sib_in[k, 0].astype(f32)).astype(bf16)
        part_far(k).start()

    relay(AB, 0)
    send_own(D)
    for copy in [load_own, load_gate, load_up] + tables:
        copy.wait()

    @each(CHUNKS + 2)
    def _(j):
        has_base = (j < CHUNKS - 1) | (j == CHUNKS)
        has_rest = j >= 2
        nb = jnp.minimum(j, CHUNKS - 1)

        @pl.when(j == 1)
        def _():
            relay(AB, 2)
            relay(D, 1)

        @pl.when(j == 2)
        def _():
            gathered(AB)
            take_ab()

        @pl.when(has_rest)
        def _():
            gated(j - 2)

        @pl.when(j == CHUNKS)
        def _():
            reduce_far(1)

        @pl.when(j == 2)
        def _():
            crossed(D)
            gathered(D)
            load_down.wait()
            take_d()

        @pl.when(has_base)
        def _():
            pass_on(nb)

        @pl.when(j == 0)
        def _():
            relay(AB, 1)

        @pl.when(has_rest)
        def _():
            projected(j - 2)

        @pl.when(has_base)
        def _():
            norm(nb)
            base(nb, 0, 3)

        @pl.when(has_rest & has_base)
        def _():
            reduce_far(j - 2)

        @pl.when(j == 0)
        def _():
            relay(D, 0)

        @pl.when(j == 1)
        def _():
            relay(D, 2)
            crossed(AB)

        @pl.when(has_base)
        def _():
            base(nb, 3, len(tiles))

    reduce_far(CHUNKS - 1)

    total = 0
    for q in range(slots):
        total = total + lengths_ref[q, r]

    @each(CHUNKS)
    def _(k):
        here = rows_of(k)
        part_far(k).wait_recv()
        branch = own_part[k, 1] + sib_in[k, 1].astype(f32) + far_in[k].astype(f32)
        branch = branch.astype(bf16).astype(f32)
        at = lax.broadcasted_iota(jnp.int32, (rc, cols), 0) + k * rc
        x = whole[m, here, :].astype(f32)
        out_ref[here, :] = jnp.where(at < total, x + branch, x).astype(out_ref.dtype)

    @each(CHUNKS)
    def _(k):
        tok_far(k, m).wait_send()
        tok_sib(k, m).wait_send()
        tok_fwd(k, far).wait_send()
        part_sib(k).wait_send()
        part_far(k).wait_send()

    for p in (AB, D):

        @each(places)
        def _(i):
            cross_copy(p, i, lane).wait_send()

            @pl.when(inner_up & (i <= place))
            def _():
                up_copy(p, i).wait_send()

            @pl.when(inner_down & (i >= place))
            def _():
                down_copy(p, i).wait_send()

        @each(groups)
        def _(g):
            af_copy(p, g).wait_send()


def on_device(
    tokens,
    norm_gain_vector,
    gate_weight,
    up_weight,
    down_weight,
    gate_up_input_maps,
    gate_up_output_maps,
    down_input_maps,
    down_output_maps,
    lengths,
    request_adapter_slot,
    selected,
):
    groups = lax.axis_size("req")
    parts = lax.axis_size("mlp")
    rows, cols = tokens.shape
    owned, rank, width = down_output_maps.shape
    inner = gate_weight.shape[1]
    slots = lengths.shape[1]
    span = slots * rank
    hwidth = width // 2
    bf16, f32 = jnp.bfloat16, jnp.float32

    rc = rows // CHUNKS
    vm, hbm = (pl.BlockSpec(memory_space=s) for s in (pltpu.VMEM, pl.ANY))
    dma = pltpu.SemaphoreType.DMA
    buffers = [
        pltpu.SMEM((slots, groups), jnp.int32),
        pltpu.SMEM((slots, groups), jnp.int32),
        pltpu.SMEM(selected.shape, jnp.int32),
        pltpu.VMEM((width, 2 * inner), bf16),
        pltpu.VMEM((inner + 2 * span, width), bf16),
        pltpu.VMEM((parts, rows, cols), bf16),
        pltpu.VMEM((CHUNKS, rc, width), bf16),
        pltpu.VMEM((CHUNKS, rc, 2 * inner), f32),
        pltpu.VMEM((rc, inner + 2 * span), bf16),
        pltpu.VMEM((groups, owned * 2 * rank, hwidth + inner), bf16),
        pltpu.VMEM((groups, owned * rank, hwidth + inner), bf16),
        pltpu.VMEM((groups, owned * 2 * rank, hwidth), bf16),
        pltpu.VMEM((groups, owned * rank, hwidth), bf16),
        pltpu.VMEM((2 * span, width), bf16),
        pltpu.VMEM((2 * span, inner), bf16),
        pltpu.VMEM((2 * span, inner), bf16),
        pltpu.VMEM((2 * span, inner), bf16),
        pltpu.VMEM((CHUNKS, 2, rc, cols), f32),
        pltpu.VMEM((CHUNKS, 2, rc, cols), bf16),
        pltpu.VMEM((CHUNKS, 2, rc, cols), bf16),
        pltpu.VMEM((CHUNKS, rc, cols), bf16),
        pltpu.VMEM((CHUNKS, rc, cols), bf16),
    ]
    held = sum(math.prod(b.shape) * jnp.dtype(b.dtype).itemsize for b in buffers)
    return pl.pallas_call(
        functools.partial(kernel, groups, owned, rank, slots),
        out_shape=jax.ShapeDtypeStruct((rows, cols), tokens.dtype),
        in_specs=[hbm] * 4 + [vm] + [hbm] * 7,
        out_specs=vm,
        scratch_shapes=buffers
        + [dma((2, groups // 2)) for _ in range(5)]
        + [dma((2, groups)) for _ in range(2)]
        + [dma((CHUNKS,)) for _ in range(10)]
        + [dma((7 + 4 * owned,))],
        compiler_params=pltpu.CompilerParams(
            collective_id=0, has_side_effects=True, vmem_limit_bytes=min(held + 6 * 1024 * 1024, 60 * 1024 * 1024)
        ),
    )(
        *(
            pltpu.with_memory_space_constraint(x, pltpu.HBM)
            for x in (
                lengths.T,
                request_adapter_slot.T,
                selected,
                tokens,
                norm_gain_vector,
                gate_weight,
                up_weight,
                down_weight,
                jnp.swapaxes(gate_up_input_maps, 1, 2),
                gate_up_output_maps.reshape(owned, 2 * rank, inner),
                jnp.swapaxes(down_input_maps, 1, 2),
                down_output_maps,
            )
        ),
    )


def solution(mesh):
    in_specs = (
        P("req", "mlp"),
        P(),
        P(None, "mlp"),
        P(None, "mlp"),
        P("mlp", None),
        P("req", None, None),
        P("req", None, None, "mlp"),
        P("req", "mlp", None),
        P("req", None, None),
        P(),
        P(),
        P(),
    )
    return jax.shard_map(
        on_device, mesh=mesh, in_specs=in_specs, out_specs=P("req", "mlp"), check_vma=False
    )
```

```python
import functools
import math

import jax
import jax.numpy as jnp
from jax import lax
from jax.experimental import pallas as pl
from jax.experimental.pallas import tpu as pltpu
from jax.sharding import PartitionSpec as P

EPSILON = 1e-06
CHUNKS = 4
MESH = pl.DeviceIdType.MESH
NT = (((1,), (1,)), ((), ()))


def kernel(groups, owned, rank, slots, *refs):
    (
        lengths_hbm, slot_hbm, chosen_hbm, tokens_ref, gain_ref, gate_ref, up_ref, down_ref,
        a_ref, b_ref, da_ref, db_ref, out_ref,
        lengths_ref, slot_ref, chosen_ref, gu_v, down_v, whole, normed, gu_sum, hidden, maps_a, maps_b, maps_d, sib_a, sib_d,
        a_sel, bg_sel, bu_sel, da_sel, own_part, sib_out, sib_in, far_out, far_in,
        up_s, dn_s, line_r, cross_s, cross_r, af_s, af_r,
        ts_s, ts_r, tc_s, tc_r, tf_s, tf_r, rs_s, rs_r, rc_s, rc_r, local_sem,
    ) = refs
    r = lax.axis_index("req")
    m = lax.axis_index("mlp")
    half = lax.rem(m, 2)
    sib = m + 1 - 2 * half
    side = m // 2
    far = m + 2 - 4 * side
    diag = sib + 2 - 4 * side
    lane = lax.rem(r, 2)
    partner = r + 1 - 2 * lane
    place = r // 2
    places = groups // 2
    rows, cols = tokens_ref.shape
    rc = rows // CHUNKS
    parts = whole.shape[0]
    width = parts * cols
    hwidth = sib_a.shape[2]
    inner = gate_ref.shape[1]
    span = slots * rank
    f32, bf16 = jnp.float32, jnp.bfloat16
    PIECES = A, B, D = 0, 1, 2
    maps = (maps_a, maps_b, maps_d)
    sibs = {A: sib_a, D: sib_d}

    def local(i, src, dst):
        return pltpu.make_async_copy(src, dst, local_sem.at[i])

    def remote(src, dst, ss, rs, axis, dev):
        return pltpu.make_async_remote_copy(
            src_ref=src,
            dst_ref=dst,
            send_sem=ss,
            recv_sem=rs,
            device_id={axis: dev},
            device_id_type=MESH,
        )

    def rows_of(k):
        return pl.ds(pl.multiple_of(k * rc, rc), rc)

    def up_copy(p, i):
        slot = maps[p].at[2 * i + lane]
        return remote(slot, slot, up_s.at[p, i], line_r.at[p, i], "req", r + 2)

    def down_copy(p, i):
        slot = maps[p].at[2 * i + lane]
        return remote(slot, slot, dn_s.at[p, i], line_r.at[p, i], "req", r - 2)

    def cross_copy(p, i, side_of):
        slot = maps[p].at[2 * i + side_of]
        return remote(slot, slot, cross_s.at[p, i], cross_r.at[p, i], "req", partner)

    def af_copy(p, g):
        return remote(
            maps[p].at[g, :, pl.ds(0, hwidth)], sibs[p].at[g], af_s.at[p, g], af_r.at[p, g], "mlp", sib
        )

    def share(p, g):
        if p in sibs:
            af_copy(p, g).start()

    def tok_sib(k, who):
        return remote(
            tokens_ref.at[rows_of(k)], whole.at[who, rows_of(k)], ts_s.at[k], ts_r.at[k], "mlp", sib
        )

    def tok_far(k, who):
        return remote(
            tokens_ref.at[rows_of(k)], whole.at[who, rows_of(k)], tc_s.at[k], tc_r.at[k], "mlp", far
        )

    def tok_fwd(k, who):
        return remote(
            whole.at[far, rows_of(k)], whole.at[who, rows_of(k)], tf_s.at[k], tf_r.at[k], "mlp", sib
        )

    def part_sib(k, h):
        return remote(sib_out.at[k, h], sib_in.at[k, h], rs_s.at[h, k], rs_r.at[h, k], "mlp", sib)

    def part_far(k):
        return remote(far_out.at[k], far_in.at[k], rc_s.at[k], rc_r.at[k], "mlp", far)

    tables = [
        local(4, lengths_hbm, lengths_ref),
        local(5, slot_hbm, slot_ref),
        local(6, chosen_hbm, chosen_ref),
    ]
    load_own = local(3, tokens_ref, whole.at[m])
    load_gate = local(0, gate_ref, gu_v.at[:, pl.ds(0, inner)])
    load_up = local(1, up_ref, gu_v.at[:, pl.ds(inner, inner)])
    load_down = local(2, down_ref, down_v.at[pl.ds(0, inner)])
    mine = pl.ds(pl.multiple_of(half * hwidth, hwidth), hwidth)
    other = pl.ds(pl.multiple_of((1 - half) * hwidth, hwidth), hwidth)
    left, right = pl.ds(0, hwidth), pl.ds(hwidth, inner)
    packs = []
    for o in range(owned):
        two, one = pl.ds(o * 2 * rank, 2 * rank), pl.ds(o * rank, rank)
        packs += [
            (a_ref.at[o, :, mine], maps_a.at[r, two]),
            (b_ref.at[o], maps_b.at[r, two]),
            (da_ref.at[o], maps_d.at[r, one, right]),
            (db_ref.at[o, :, mine], maps_d.at[r, one, left]),
        ]
    packs = [local(7 + i, src, dst) for i, (src, dst) in enumerate(packs)]
    for copy in packs:
        copy.start()

    barrier = pltpu.get_barrier_semaphore()

    def greet(axis, dev):
        pl.semaphore_signal(barrier, inc=1, device_id={axis: dev}, device_id_type=MESH)

    greet("mlp", sib)
    greet("mlp", far)
    greet("req", partner)
    inner_up = place < places - 1
    inner_down = place > 0
    @pl.when(inner_up)
    def _():
        greet("req", r + 2)

    @pl.when(inner_down)
    def _():
        greet("req", r - 2)

    below = (place + places - 1) // places
    above = (2 * (places - 1) - place) // places
    pl.semaphore_wait(barrier, 3 + below + above)

    def each(n, start=0):
        def deco(f):
            def body(i, carry):
                f(i)
                return carry

            lax.fori_loop(start, n, body, 0)

        return deco

    @each(CHUNKS)
    def _(k):
        tok_far(k, m).start()
        tok_sib(k, m).start()

    for copy in packs:
        copy.wait()

    def send_own(p):
        @pl.when(inner_up)
        def _():
            up_copy(p, place).start()

        @pl.when(inner_down)
        def _():
            down_copy(p, place).start()

        cross_copy(p, place, lane).start()
        share(p, r)

    for p in PIECES:
        send_own(p)
    for copy in [load_own, load_gate, load_up, load_down] + tables:
        copy.start()

    def relay(p, part):
        def body(d, carry):
            @pl.when(place - d >= 0)
            def _():
                i = place - d
                up_copy(p, i).wait_recv()

                @pl.when(inner_up)
                def _():
                    up_copy(p, i).start()

                cross_copy(p, i, lane).start()
                share(p, 2 * i + lane)

            @pl.when(place + d < places)
            def _():
                i = place + d
                down_copy(p, i).wait_recv()

                @pl.when(inner_down)
                def _():
                    down_copy(p, i).start()

                cross_copy(p, i, lane).start()
                share(p, 2 * i + lane)

            return carry

        first = 1 + (places - 1) * part // 3
        last = 1 + (places - 1) * (part + 1) // 3
        lax.fori_loop(first, last, body, 0)

    def crossed(p):
        @each(places)
        def _(i):
            cross_copy(p, i, 1 - lane).wait_recv()
            share(p, 2 * i + 1 - lane)

    def gathered(p):
        @each(groups)
        def _(g):
            af_copy(p, g).wait_recv()

    def pick(q):
        chosen = chosen_ref[slot_ref[q, r]]
        if owned > 1:
            return chosen // owned, lax.rem(chosen, owned)
        return chosen, 0

    def take_ab():
        crossed_cols = ((mine, maps_a), (other, sib_a))
        for q in range(slots):
            g, o = pick(q)
            one, two = pl.ds(o * 2 * rank, rank), pl.ds(o * 2 * rank + rank, rank)
            at, at2 = pl.ds(q * rank, rank), pl.ds(span + q * rank, rank)
            for dst, part in crossed_cols:
                a_sel[at, dst] = part[g, one, :]
                a_sel[at2, dst] = part[g, two, :]
            bg_sel[at, :] = maps_b[g, one, :]
            bu_sel[at2, :] = maps_b[g, two, :]

    def take_d():
        for q in range(slots):
            g, o = pick(q)
            one = pl.ds(o * rank, rank)
            at, at2 = pl.ds(q * rank, rank), pl.ds(span + q * rank, rank)
            for dst, part in ((mine, maps_d), (other, sib_d)):
                db = part[g, one, 0:hwidth]
                down_v[pl.ds(inner + q * rank, rank), dst] = db
                down_v[pl.ds(inner + span + q * rank, rank), dst] = db
            da = maps_d[g, one, hwidth : hwidth + inner]
            da_sel[at, :] = da
            da_sel[at2, :] = da

    def live_rows(k):
        column = lax.broadcasted_iota(jnp.int32, (1, 2 * span), 1)
        column = jnp.where(column < span, column, column - span)
        low = jnp.zeros((1, 2 * span), jnp.int32)
        high = jnp.zeros((1, 2 * span), jnp.int32)
        end = 0
        for q in range(slots):
            own_q = (column >= q * rank) & (column < (q + 1) * rank)
            low = jnp.where(own_q, end, low)
            end = end + lengths_ref[q, r]
            high = jnp.where(own_q, end, high)
        at = lax.broadcasted_iota(jnp.int32, (rc, 2 * span), 0) + k * rc
        return (at >= low) & (at < high)

    def pass_on(k):
        tok_far(k, far).wait_recv()
        tok_fwd(k, far).start()

    def norm(k):
        here = rows_of(k)
        tok_sib(k, sib).wait_recv()
        tok_fwd(k, diag).wait_recv()
        gain_row = gain_ref[...].astype(f32).reshape(1, -1)
        squares = jnp.zeros((rc, 1), f32)
        for b in range(parts):
            x = whole[b, here, :].astype(f32)
            squares += jnp.sum(x * x, axis=1, keepdims=True)
        scale = lax.rsqrt(squares / width + EPSILON)
        for b in range(parts):
            x = whole[b, here, :].astype(f32)
            gain = gain_row[:, b * cols : (b + 1) * cols]
            normed[k, :, b * cols : (b + 1) * cols] = (x * scale * gain).astype(bf16)

    tiles = list(range(0, 2 * inner, 256))

    def base(k, first, last):
        for n0 in tiles[first:last]:
            n1 = min(n0 + 256, 2 * inner)
            gu_sum[k, :, n0:n1] = jnp.dot(normed[k], gu_v[:, n0:n1], preferred_element_type=f32)

    def gated(k):
        live = live_rows(k)
        low_rank = lax.dot_general(normed[k], a_sel[...], NT, preferred_element_type=f32)
        low_rank = jnp.where(live, low_rank, 0.0).astype(bf16)
        for n0 in range(0, inner, 256):
            n1 = min(n0 + 256, inner)
            g = gu_sum[k, :, n0:n1]
            g += jnp.dot(low_rank, bg_sel[:, n0:n1], preferred_element_type=f32)
            u = gu_sum[k, :, inner + n0 : inner + n1]
            u += jnp.dot(low_rank, bu_sel[:, n0:n1], preferred_element_type=f32)
            hidden[lax.rem(k, 2), :, n0:n1] = (jax.nn.silu(g) * u).astype(bf16)

    def projected(k):
        live = live_rows(k)
        down_rank = lax.dot_general(hidden[lax.rem(k, 2), :, :inner], da_sel[...], NT, preferred_element_type=f32)
        down_rank = jnp.where(live, down_rank, 0.0)
        coarse = down_rank.astype(bf16).astype(f32)
        column = lax.broadcasted_iota(jnp.int32, (rc, 2 * span), 1)
        down_rank = jnp.where(column < span, coarse, down_rank - coarse).astype(bf16)
        hidden[lax.rem(k, 2), :, inner:] = down_rank

        def part_of(b):
            there = pl.ds(pl.multiple_of(b * cols, cols), cols)
            return jnp.dot(hidden[lax.rem(k, 2)], down_v[:, there], preferred_element_type=f32)

        sib_out[k, 0] = part_of(diag).astype(bf16)
        part_sib(k, 0).start()
        sib_out[k, 1] = part_of(sib).astype(bf16)
        part_sib(k, 1).start()
        own_part[k, 0] = part_of(far)
        own_part[k, 1] = part_of(m)

    def reduce_far(k):
        part_sib(k, 0).wait_recv()
        far_out[k] = (own_part[k, 0] + sib_in[k, 0].astype(f32)).astype(bf16)
        part_far(k).start()

    for p in PIECES:
        relay(p, 0)
    relay(A, 1)
    bg_sel[...] = jnp.zeros_like(bg_sel)
    bu_sel[...] = jnp.zeros_like(bu_sel)
    for copy in [load_own, load_gate, load_up] + tables:
        copy.wait()

    @each(7)
    def _(j):
        def at(step):
            return pl.when(j == step)

        has_base = (j < 2) | (j == 4) | (j == 5)
        has_gated = (j == 2) | (j == 3) | (j >= 5)
        has_rest = j >= 3
        kb = jnp.where(j < 2, j, j - 2)
        kg = jnp.where(j < 4, j - 2, j - 3)
        kp = j - 3

        @at(1)
        def _():
            relay(B, 2)

        @pl.when(j < 2)
        def _():
            pass_on(j)

        @at(0)
        def _():
            relay(B, 1)

        @at(1)
        def _():
            relay(D, 2)

        @pl.when(has_base)
        def _():
            norm(kb)

        @pl.when((j == 4) | (j == 5))
        def _():
            reduce_far(j - 4)

        @pl.when(has_base)
        def _():
            base(kb, 0, 3)

        @at(0)
        def _():
            relay(D, 1)

        @pl.when(has_base)
        def _():
            base(kb, 3, len(tiles))

        @at(0)
        def _():
            relay(A, 2)

        @at(1)
        def _():
            crossed(A)

        @at(2)
        def _():
            crossed(B)
            gathered(A)
            take_ab()

        @pl.when(has_gated)
        def _():
            gated(kg)

        @at(2)
        def _():
            pass_on(2)
            crossed(D)

        @at(3)
        def _():
            gathered(D)
            load_down.wait()
            take_d()

        @at(4)
        def _():
            pass_on(3)

        @at(6)
        def _():
            reduce_far(2)

        @pl.when(has_rest)
        def _():
            projected(kp)

    reduce_far(3)

    total = 0
    for q in range(slots):
        total = total + lengths_ref[q, r]

    @each(CHUNKS)
    def _(k):
        here = rows_of(k)
        part_sib(k, 1).wait_recv()
        part_far(k).wait_recv()
        branch = own_part[k, 1] + sib_in[k, 1].astype(f32) + far_in[k].astype(f32)
        branch = branch.astype(bf16).astype(f32)
        at = lax.broadcasted_iota(jnp.int32, (rc, cols), 0) + k * rc
        x = whole[m, here, :].astype(f32)
        out_ref[here, :] = jnp.where(at < total, x + branch, x).astype(out_ref.dtype)

    @each(CHUNKS)
    def _(k):
        tok_far(k, m).wait_send()
        tok_sib(k, m).wait_send()
        tok_fwd(k, far).wait_send()
        part_sib(k, 0).wait_send()
        part_sib(k, 1).wait_send()
        part_far(k).wait_send()

    for p in PIECES:

        @each(places)
        def _(i):
            cross_copy(p, i, lane).wait_send()

            @pl.when(inner_up & (i <= place))
            def _():
                up_copy(p, i).wait_send()

            @pl.when(inner_down & (i >= place))
            def _():
                down_copy(p, i).wait_send()

        if p in sibs:

            @each(groups)
            def _(g):
                af_copy(p, g).wait_send()


def on_device(
    tokens,
    norm_gain_vector,
    gate_weight,
    up_weight,
    down_weight,
    gate_up_input_maps,
    gate_up_output_maps,
    down_input_maps,
    down_output_maps,
    lengths,
    request_adapter_slot,
    selected,
):
    groups = lax.axis_size("req")
    parts = lax.axis_size("mlp")
    rows, cols = tokens.shape
    owned, rank, width = down_output_maps.shape
    inner = gate_weight.shape[1]
    slots = lengths.shape[1]
    span = slots * rank
    hwidth = width // 2
    bf16, f32 = jnp.bfloat16, jnp.float32

    rc = rows // CHUNKS
    vm, hbm = (pl.BlockSpec(memory_space=s) for s in (pltpu.VMEM, pl.ANY))
    dma = pltpu.SemaphoreType.DMA
    buffers = [
        pltpu.SMEM((slots, groups), jnp.int32),
        pltpu.SMEM((slots, groups), jnp.int32),
        pltpu.SMEM(selected.shape, jnp.int32),
        pltpu.VMEM((width, 2 * inner), bf16),
        pltpu.VMEM((inner + 2 * span, width), bf16),
        pltpu.VMEM((parts, rows, cols), bf16),
        pltpu.VMEM((CHUNKS, rc, width), bf16),
        pltpu.VMEM((CHUNKS, rc, 2 * inner), f32),
        pltpu.VMEM((2, rc, inner + 2 * span), bf16),
        pltpu.VMEM((groups, owned * 2 * rank, hwidth), bf16),
        pltpu.VMEM((groups, owned * 2 * rank, inner), bf16),
        pltpu.VMEM((groups, owned * rank, hwidth + inner), bf16),
        pltpu.VMEM((groups, owned * 2 * rank, hwidth), bf16),
        pltpu.VMEM((groups, owned * rank, hwidth), bf16),
        pltpu.VMEM((2 * span, width), bf16),
        pltpu.VMEM((2 * span, inner), bf16),
        pltpu.VMEM((2 * span, inner), bf16),
        pltpu.VMEM((2 * span, inner), bf16),
        pltpu.VMEM((CHUNKS, 2, rc, cols), f32),
        pltpu.VMEM((CHUNKS, 2, rc, cols), bf16),
        pltpu.VMEM((CHUNKS, 2, rc, cols), bf16),
        pltpu.VMEM((CHUNKS, rc, cols), bf16),
        pltpu.VMEM((CHUNKS, rc, cols), bf16),
    ]
    held = sum(math.prod(b.shape) * jnp.dtype(b.dtype).itemsize for b in buffers)
    return pl.pallas_call(
        functools.partial(kernel, groups, owned, rank, slots),
        out_shape=jax.ShapeDtypeStruct((rows, cols), tokens.dtype),
        in_specs=[hbm] * 4 + [vm] + [hbm] * 7,
        out_specs=vm,
        scratch_shapes=buffers
        + [dma((3, groups // 2)) for _ in range(5)]
        + [dma((3, groups)) for _ in range(2)]
        + [dma((CHUNKS,)) for _ in range(6)]
        + [dma((2, CHUNKS)) for _ in range(2)]
        + [dma((CHUNKS,)) for _ in range(2)]
        + [dma((7 + 4 * owned,))],
        compiler_params=pltpu.CompilerParams(
            collective_id=0, has_side_effects=True, vmem_limit_bytes=min(held + 6 * 1024 * 1024, 60 * 1024 * 1024)
        ),
    )(
        *(
            pltpu.with_memory_space_constraint(x, pltpu.HBM)
            for x in (
                lengths.T,
                request_adapter_slot.T,
                selected,
                tokens,
                norm_gain_vector,
                gate_weight,
                up_weight,
                down_weight,
                jnp.swapaxes(gate_up_input_maps, 1, 2),
                gate_up_output_maps.reshape(owned, 2 * rank, inner),
                jnp.swapaxes(down_input_maps, 1, 2),
                down_output_maps,
            )
        ),
    )


def solution(mesh):
    in_specs = (
        P("req", "mlp"),
        P(),
        P(None, "mlp"),
        P(None, "mlp"),
        P("mlp", None),
        P("req", None, None),
        P("req", None, None, "mlp"),
        P("req", "mlp", None),
        P("req", None, None),
        P(),
        P(),
        P(),
    )
    return jax.shard_map(
        on_device, mesh=mesh, in_specs=in_specs, out_specs=P("req", "mlp"), check_vma=False
    )
```

```python
import functools
import math

import jax
import jax.numpy as jnp
from jax import lax
from jax.experimental import pallas as pl
from jax.experimental.pallas import tpu as pltpu
from jax.sharding import PartitionSpec as P

EPSILON = 1e-06
CHUNKS = 4
MESH = pl.DeviceIdType.MESH
NT = (((1,), (1,)), ((), ()))


def kernel(groups, owned, rank, slots, *refs):
    (
        lengths_hbm, slot_hbm, chosen_hbm, tokens_ref, gain_hbm, gate_ref, up_ref, down_ref,
        a_ref, b_ref, da_ref, db_ref, out_ref,
        lengths_ref, slot_ref, chosen_ref, gain_ref, gu_v, down_v, whole, normed, gu_sum, hidden, maps_a, maps_b, maps_d, sib_a, sib_d,
        a_sel, bg_sel, bu_sel, da_sel, own_part, sib_out, sib_in, far_out, far_in,
        up_s, dn_s, line_r, cross_s, cross_r, af_s, af_r,
        ts_s, ts_r, tc_s, tc_r, tf_s, tf_r, rs_s, rs_r, rc_s, rc_r, local_sem,
    ) = refs
    r = lax.axis_index("req")
    m = lax.axis_index("mlp")
    half = lax.rem(m, 2)
    sib = m + 1 - 2 * half
    side = m // 2
    far = m + 2 - 4 * side
    diag = sib + 2 - 4 * side
    lane = lax.rem(r, 2)
    partner = r + 1 - 2 * lane
    place = r // 2
    places = groups // 2
    rows, cols = tokens_ref.shape
    rc = rows // CHUNKS
    parts = whole.shape[0]
    width = parts * cols
    hwidth = sib_a.shape[2]
    inner = gate_ref.shape[1]
    span = slots * rank
    f32, bf16 = jnp.float32, jnp.bfloat16
    PIECES = A, D, B = 0, 1, 2
    maps = (maps_a, maps_d, maps_b)
    sibs = {A: sib_a, D: sib_d}

    def local(i, src, dst):
        return pltpu.make_async_copy(src, dst, local_sem.at[i])

    def remote(src, dst, ss, rs, axis, dev):
        return pltpu.make_async_remote_copy(
            src_ref=src,
            dst_ref=dst,
            send_sem=ss,
            recv_sem=rs,
            device_id={axis: dev},
            device_id_type=MESH,
        )

    def rows_of(k):
        return pl.ds(pl.multiple_of(k * rc, rc), rc)

    def up_copy(p, i):
        slot = maps[p].at[2 * i + lane]
        return remote(slot, slot, up_s.at[p, i], line_r.at[p, i], "req", r + 2)

    def down_copy(p, i):
        slot = maps[p].at[2 * i + lane]
        return remote(slot, slot, dn_s.at[p, i], line_r.at[p, i], "req", r - 2)

    def cross_copy(p, i, side_of):
        slot = maps[p].at[2 * i + side_of]
        return remote(slot, slot, cross_s.at[p, i], cross_r.at[p, i], "req", partner)

    def af_copy(p, g):
        return remote(
            maps[p].at[g, :, pl.ds(0, hwidth)], sibs[p].at[g], af_s.at[p, g], af_r.at[p, g], "mlp", sib
        )

    def share(p, g):
        if p in sibs:
            af_copy(p, g).start()

    def tok_sib(k, who):
        return remote(
            tokens_ref.at[rows_of(k)], whole.at[who, rows_of(k)], ts_s.at[k], ts_r.at[k], "mlp", sib
        )

    def tok_far(k, who):
        return remote(
            tokens_ref.at[rows_of(k)], whole.at[who, rows_of(k)], tc_s.at[k], tc_r.at[k], "mlp", far
        )

    def tok_fwd(k, who):
        return remote(
            whole.at[far, rows_of(k)], whole.at[who, rows_of(k)], tf_s.at[k], tf_r.at[k], "mlp", sib
        )

    def part_sib(k, h):
        return remote(sib_out.at[k, h], sib_in.at[k, h], rs_s.at[h, k], rs_r.at[h, k], "mlp", sib)

    def part_far(k):
        return remote(far_out.at[k], far_in.at[k], rc_s.at[k], rc_r.at[k], "mlp", far)

    tables = [
        local(4, lengths_hbm, lengths_ref),
        local(5, slot_hbm, slot_ref),
        local(6, chosen_hbm, chosen_ref),
        local(7, gain_hbm, gain_ref),
    ]
    load_own = local(3, tokens_ref, whole.at[m])
    load_gate = local(0, gate_ref, gu_v.at[:, pl.ds(0, inner)])
    load_up = local(1, up_ref, gu_v.at[:, pl.ds(inner, inner)])
    load_down = local(2, down_ref, down_v.at[pl.ds(0, inner)])
    mine = pl.ds(pl.multiple_of(half * hwidth, hwidth), hwidth)
    other = pl.ds(pl.multiple_of((1 - half) * hwidth, hwidth), hwidth)
    left, right = pl.ds(0, hwidth), pl.ds(hwidth, inner)
    packs = []
    for o in range(owned):
        two, one = pl.ds(o * 2 * rank, 2 * rank), pl.ds(o * rank, rank)
        packs += [
            (a_ref.at[o, :, mine], maps_a.at[r, two]),
            (b_ref.at[o], maps_b.at[r, two]),
            (da_ref.at[o], maps_d.at[r, one, right]),
            (db_ref.at[o, :, mine], maps_d.at[r, one, left]),
        ]
    packs = [local(8 + i, src, dst) for i, (src, dst) in enumerate(packs)]

    barrier = pltpu.get_barrier_semaphore()

    def greet(axis, dev):
        pl.semaphore_signal(barrier, inc=1, device_id={axis: dev}, device_id_type=MESH)

    greet("mlp", sib)
    greet("mlp", far)
    greet("req", partner)
    inner_up = place < places - 1
    inner_down = place > 0
    @pl.when(inner_up)
    def _():
        greet("req", r + 2)

    @pl.when(inner_down)
    def _():
        greet("req", r - 2)

    for copy in packs:
        copy.start()
    below = (place + places - 1) // places
    above = (2 * (places - 1) - place) // places
    pl.semaphore_wait(barrier, 3 + below + above)

    def each(n, start=0):
        def deco(f):
            def body(i, carry):
                f(i)
                return carry

            lax.fori_loop(start, n, body, 0)

        return deco

    @each(CHUNKS)
    def _(k):
        tok_far(k, m).start()
        tok_sib(k, m).start()

    for copy in packs:
        copy.wait()

    def send_own(p):
        @pl.when(inner_up)
        def _():
            up_copy(p, place).start()

        @pl.when(inner_down)
        def _():
            down_copy(p, place).start()

        cross_copy(p, place, lane).start()
        share(p, r)

    for p in PIECES:
        send_own(p)
    for copy in [load_own, load_gate, load_up, load_down] + tables:
        copy.start()

    def relay(p, part):
        def body(d, carry):
            @pl.when(place - d >= 0)
            def _():
                i = place - d
                up_copy(p, i).wait_recv()

                @pl.when(inner_up)
                def _():
                    up_copy(p, i).start()

                cross_copy(p, i, lane).start()
                share(p, 2 * i + lane)

            @pl.when(place + d < places)
            def _():
                i = place + d
                down_copy(p, i).wait_recv()

                @pl.when(inner_down)
                def _():
                    down_copy(p, i).start()

                cross_copy(p, i, lane).start()
                share(p, 2 * i + lane)

            return carry

        first = 1 + (places - 1) * part // 3
        last = 1 + (places - 1) * (part + 1) // 3
        lax.fori_loop(first, last, body, 0)

    def crossed(p):
        @each(places)
        def _(i):
            cross_copy(p, i, 1 - lane).wait_recv()
            share(p, 2 * i + 1 - lane)

    def gathered(p):
        @each(groups)
        def _(g):
            af_copy(p, g).wait_recv()

    def pick(q):
        chosen = chosen_ref[slot_ref[q, r]]
        if owned > 1:
            return chosen // owned, lax.rem(chosen, owned)
        return chosen, 0

    def take_ab():
        crossed_cols = ((mine, maps_a), (other, sib_a))
        for q in range(slots):
            g, o = pick(q)
            one, two = pl.ds(o * 2 * rank, rank), pl.ds(o * 2 * rank + rank, rank)
            at, at2 = pl.ds(q * rank, rank), pl.ds(span + q * rank, rank)
            for dst, part in crossed_cols:
                a_sel[at, dst] = part[g, one, :]
                a_sel[at2, dst] = part[g, two, :]
            bg_sel[at, :] = maps_b[g, one, :]
            bu_sel[at2, :] = maps_b[g, two, :]

    def take_d():
        for q in range(slots):
            g, o = pick(q)
            one = pl.ds(o * rank, rank)
            at, at2 = pl.ds(q * rank, rank), pl.ds(span + q * rank, rank)
            for dst, part in ((mine, maps_d), (other, sib_d)):
                db = part[g, one, 0:hwidth]
                down_v[pl.ds(inner + q * rank, rank), dst] = db
                down_v[pl.ds(inner + span + q * rank, rank), dst] = db
            da = maps_d[g, one, hwidth : hwidth + inner]
            da_sel[at, :] = da
            da_sel[at2, :] = da

    def live_rows(k):
        column = lax.broadcasted_iota(jnp.int32, (1, 2 * span), 1)
        column = jnp.where(column < span, column, column - span)
        low = jnp.zeros((1, 2 * span), jnp.int32)
        high = jnp.zeros((1, 2 * span), jnp.int32)
        end = 0
        for q in range(slots):
            own_q = (column >= q * rank) & (column < (q + 1) * rank)
            low = jnp.where(own_q, end, low)
            end = end + lengths_ref[q, r]
            high = jnp.where(own_q, end, high)
        at = lax.broadcasted_iota(jnp.int32, (rc, 2 * span), 0) + k * rc
        return (at >= low) & (at < high)

    def pass_on(k):
        tok_far(k, far).wait_recv()
        tok_fwd(k, far).start()

    def norm(k):
        here = rows_of(k)
        tok_sib(k, sib).wait_recv()
        tok_fwd(k, diag).wait_recv()
        gain_row = gain_ref[...].astype(f32).reshape(1, -1)
        squares = jnp.zeros((rc, 1), f32)
        for b in range(parts):
            x = whole[b, here, :].astype(f32)
            squares += jnp.sum(x * x, axis=1, keepdims=True)
        scale = lax.rsqrt(squares / width + EPSILON)
        for b in range(parts):
            x = whole[b, here, :].astype(f32)
            gain = gain_row[:, b * cols : (b + 1) * cols]
            normed[k, :, b * cols : (b + 1) * cols] = (x * scale * gain).astype(bf16)

    tiles = list(range(0, 2 * inner, 256))

    def base(k, first, last):
        for n0 in tiles[first:last]:
            n1 = min(n0 + 256, 2 * inner)
            gu_sum[k, :, n0:n1] = jnp.dot(normed[k], gu_v[:, n0:n1], preferred_element_type=f32)

    def gated(k):
        live = live_rows(k)
        low_rank = lax.dot_general(normed[k], a_sel[...], NT, preferred_element_type=f32)
        low_rank = jnp.where(live, low_rank, 0.0).astype(bf16)
        for n0 in range(0, inner, 256):
            n1 = min(n0 + 256, inner)
            g = gu_sum[k, :, n0:n1]
            g += jnp.dot(low_rank, bg_sel[:, n0:n1], preferred_element_type=f32)
            u = gu_sum[k, :, inner + n0 : inner + n1]
            u += jnp.dot(low_rank, bu_sel[:, n0:n1], preferred_element_type=f32)
            hidden[:, n0:n1] = (jax.nn.silu(g) * u).astype(bf16)

    def projected(k):
        live = live_rows(k)
        down_rank = lax.dot_general(hidden[:, :inner], da_sel[...], NT, preferred_element_type=f32)
        down_rank = jnp.where(live, down_rank, 0.0)
        coarse = down_rank.astype(bf16).astype(f32)
        column = lax.broadcasted_iota(jnp.int32, (rc, 2 * span), 1)
        down_rank = jnp.where(column < span, coarse, down_rank - coarse).astype(bf16)
        hidden[:, inner:] = down_rank

        def part_of(b):
            there = pl.ds(pl.multiple_of(b * cols, cols), cols)
            return jnp.dot(hidden[...], down_v[:, there], preferred_element_type=f32)

        sib_out[k, 0] = part_of(diag).astype(bf16)
        part_sib(k, 0).start()
        sib_out[k, 1] = part_of(sib).astype(bf16)
        part_sib(k, 1).start()
        own_part[k, 0] = part_of(far)
        own_part[k, 1] = part_of(m)

    def reduce_far(k):
        part_sib(k, 0).wait_recv()
        far_out[k] = (own_part[k, 0] + sib_in[k, 0].astype(f32)).astype(bf16)
        part_far(k).start()

    for p in PIECES:
        relay(p, 0)
    relay(A, 1)
    bg_sel[...] = jnp.zeros_like(bg_sel)
    bu_sel[...] = jnp.zeros_like(bu_sel)
    for copy in [load_own, load_gate, load_up] + tables:
        copy.wait()

    @each(CHUNKS + 2)
    def _(j):
        def at(step):
            return pl.when(j == step)

        has_base = (j < 2) | (j == 3) | (j == 4)
        has_rest = j >= 2
        kb = jnp.where(j < 2, j, j - 1)
        kr = j - 2

        @at(1)
        def _():
            relay(D, 2)

        @pl.when(j < 2)
        def _():
            pass_on(j)

        @at(0)
        def _():
            relay(D, 1)

        @at(1)
        def _():
            relay(B, 2)

        @pl.when(has_base)
        def _():
            norm(kb)

        @pl.when(has_base & has_rest)
        def _():
            reduce_far(j - 3)

        @pl.when(has_base)
        def _():
            base(kb, 0, 3)

        @at(0)
        def _():
            relay(B, 1)

        @pl.when(has_base)
        def _():
            base(kb, 3, len(tiles))

        @at(0)
        def _():
            relay(A, 2)

        @at(1)
        def _():
            crossed(A)
            crossed(D)

        @at(2)
        def _():
            crossed(B)
            gathered(A)
            take_ab()

        @pl.when(has_rest)
        def _():
            gated(kr)

        @at(2)
        def _():
            pass_on(2)
            gathered(D)
            load_down.wait()
            take_d()

        @at(3)
        def _():
            pass_on(3)

        @at(5)
        def _():
            reduce_far(2)

        @pl.when(has_rest)
        def _():
            projected(kr)

    reduce_far(3)

    total = 0
    for q in range(slots):
        total = total + lengths_ref[q, r]

    @each(CHUNKS)
    def _(k):
        here = rows_of(k)
        part_sib(k, 1).wait_recv()
        part_far(k).wait_recv()
        branch = own_part[k, 1] + sib_in[k, 1].astype(f32) + far_in[k].astype(f32)
        branch = branch.astype(bf16).astype(f32)
        at = lax.broadcasted_iota(jnp.int32, (rc, cols), 0) + k * rc
        x = whole[m, here, :].astype(f32)
        out_ref[here, :] = jnp.where(at < total, x + branch, x).astype(out_ref.dtype)

    @each(CHUNKS)
    def _(k):
        tok_far(k, m).wait_send()
        tok_sib(k, m).wait_send()
        tok_fwd(k, far).wait_send()
        part_sib(k, 0).wait_send()
        part_sib(k, 1).wait_send()
        part_far(k).wait_send()

    for p in PIECES:

        @each(places)
        def _(i):
            cross_copy(p, i, lane).wait_send()

            @pl.when(inner_up & (i <= place))
            def _():
                up_copy(p, i).wait_send()

            @pl.when(inner_down & (i >= place))
            def _():
                down_copy(p, i).wait_send()

        if p in sibs:

            @each(groups)
            def _(g):
                af_copy(p, g).wait_send()


def on_device(
    tokens,
    norm_gain_vector,
    gate_weight,
    up_weight,
    down_weight,
    gate_up_input_maps,
    gate_up_output_maps,
    down_input_maps,
    down_output_maps,
    lengths,
    request_adapter_slot,
    selected,
):
    groups = lax.axis_size("req")
    parts = lax.axis_size("mlp")
    rows, cols = tokens.shape
    owned, rank, width = down_output_maps.shape
    inner = gate_weight.shape[1]
    slots = lengths.shape[1]
    span = slots * rank
    hwidth = width // 2
    bf16, f32 = jnp.bfloat16, jnp.float32

    rc = rows // CHUNKS
    vm, hbm = (pl.BlockSpec(memory_space=s) for s in (pltpu.VMEM, pl.ANY))
    dma = pltpu.SemaphoreType.DMA
    buffers = [
        pltpu.SMEM((slots, groups), jnp.int32),
        pltpu.SMEM((slots, groups), jnp.int32),
        pltpu.SMEM(selected.shape, jnp.int32),
        pltpu.VMEM(norm_gain_vector.shape, bf16),
        pltpu.VMEM((width, 2 * inner), bf16),
        pltpu.VMEM((inner + 2 * span, width), bf16),
        pltpu.VMEM((parts, rows, cols), bf16),
        pltpu.VMEM((CHUNKS, rc, width), bf16),
        pltpu.VMEM((CHUNKS, rc, 2 * inner), f32),
        pltpu.VMEM((rc, inner + 2 * span), bf16),
        pltpu.VMEM((groups, owned * 2 * rank, hwidth), bf16),
        pltpu.VMEM((groups, owned * 2 * rank, inner), bf16),
        pltpu.VMEM((groups, owned * rank, hwidth + inner), bf16),
        pltpu.VMEM((groups, owned * 2 * rank, hwidth), bf16),
        pltpu.VMEM((groups, owned * rank, hwidth), bf16),
        pltpu.VMEM((2 * span, width), bf16),
        pltpu.VMEM((2 * span, inner), bf16),
        pltpu.VMEM((2 * span, inner), bf16),
        pltpu.VMEM((2 * span, inner), bf16),
        pltpu.VMEM((CHUNKS, 2, rc, cols), f32),
        pltpu.VMEM((CHUNKS, 2, rc, cols), bf16),
        pltpu.VMEM((CHUNKS, 2, rc, cols), bf16),
        pltpu.VMEM((CHUNKS, rc, cols), bf16),
        pltpu.VMEM((CHUNKS, rc, cols), bf16),
    ]
    held = sum(math.prod(b.shape) * jnp.dtype(b.dtype).itemsize for b in buffers)
    return pl.pallas_call(
        functools.partial(kernel, groups, owned, rank, slots),
        out_shape=jax.ShapeDtypeStruct((rows, cols), tokens.dtype),
        in_specs=[hbm] * 12,
        out_specs=vm,
        scratch_shapes=buffers
        + [dma((3, groups // 2)) for _ in range(5)]
        + [dma((3, groups)) for _ in range(2)]
        + [dma((CHUNKS,)) for _ in range(6)]
        + [dma((2, CHUNKS)) for _ in range(2)]
        + [dma((CHUNKS,)) for _ in range(2)]
        + [dma((8 + 4 * owned,))],
        compiler_params=pltpu.CompilerParams(
            collective_id=0, has_side_effects=True, vmem_limit_bytes=min(held + 6 * 1024 * 1024, 60 * 1024 * 1024)
        ),
    )(
        *(
            pltpu.with_memory_space_constraint(x, pltpu.HBM)
            for x in (
                lengths.T,
                request_adapter_slot.T,
                selected,
                tokens,
                norm_gain_vector,
                gate_weight,
                up_weight,
                down_weight,
                jnp.swapaxes(gate_up_input_maps, 1, 2),
                gate_up_output_maps.reshape(owned, 2 * rank, inner),
                jnp.swapaxes(down_input_maps, 1, 2),
                down_output_maps,
            )
        ),
    )


def solution(mesh):
    in_specs = (
        P("req", "mlp"),
        P(),
        P(None, "mlp"),
        P(None, "mlp"),
        P("mlp", None),
        P("req", None, None),
        P("req", None, None, "mlp"),
        P("req", "mlp", None),
        P("req", None, None),
        P(),
        P(),
        P(),
    )
    return jax.shard_map(
        on_device, mesh=mesh, in_specs=in_specs, out_specs=P("req", "mlp"), check_vma=False
    )
```

```python
import functools
import math

import jax
import jax.numpy as jnp
from jax import lax
from jax.experimental import pallas as pl
from jax.experimental.pallas import tpu as pltpu
from jax.sharding import PartitionSpec as P

EPSILON = 1e-06
CHUNKS = 4
MESH = pl.DeviceIdType.MESH
NT = (((1,), (1,)), ((), ()))


def kernel(groups, owned, rank, slots, *refs):
    (
        lengths_hbm, slot_hbm, chosen_hbm, tokens_ref, gain_hbm, gate_ref, up_ref, down_ref,
        a_ref, b_ref, da_ref, db_ref, out_ref,
        lengths_ref, slot_ref, chosen_ref, gain_ref, gu_v, down_v, whole, normed, gu_sum, hidden, maps_a, maps_b, maps_d, sib_a, sib_d,
        a_sel, bg_sel, bu_sel, da_sel, own_part, sib_out, sib_in, far_out, far_in,
        up_s, dn_s, line_r, cross_s, cross_r, af_s, af_r,
        ts_s, ts_r, tc_s, tc_r, tf_s, tf_r, rs_s, rs_r, rc_s, rc_r, local_sem,
    ) = refs
    r = lax.axis_index("req")
    m = lax.axis_index("mlp")
    half = lax.rem(m, 2)
    sib = m + 1 - 2 * half
    side = m // 2
    far = m + 2 - 4 * side
    diag = sib + 2 - 4 * side
    lane = lax.rem(r, 2)
    partner = r + 1 - 2 * lane
    place = r // 2
    places = groups // 2
    rows, cols = tokens_ref.shape
    rc = rows // CHUNKS
    parts = whole.shape[0]
    width = parts * cols
    hwidth = sib_a.shape[2]
    inner = gate_ref.shape[1]
    span = slots * rank
    f32, bf16 = jnp.float32, jnp.bfloat16
    PIECES = A, D, B = 0, 1, 2
    maps = (maps_a, maps_d, maps_b)
    sibs = {A: sib_a, D: sib_d}

    def local(i, src, dst):
        return pltpu.make_async_copy(src, dst, local_sem.at[i])

    def remote(src, dst, ss, rs, axis, dev):
        return pltpu.make_async_remote_copy(
            src_ref=src,
            dst_ref=dst,
            send_sem=ss,
            recv_sem=rs,
            device_id={axis: dev},
            device_id_type=MESH,
        )

    def rows_of(k):
        return pl.ds(pl.multiple_of(k * rc, rc), rc)

    def up_copy(p, i):
        slot = maps[p].at[2 * i + lane]
        return remote(slot, slot, up_s.at[p, i], line_r.at[p, i], "req", r + 2)

    def down_copy(p, i):
        slot = maps[p].at[2 * i + lane]
        return remote(slot, slot, dn_s.at[p, i], line_r.at[p, i], "req", r - 2)

    def cross_copy(p, i, side_of):
        slot = maps[p].at[2 * i + side_of]
        return remote(slot, slot, cross_s.at[p, i], cross_r.at[p, i], "req", partner)

    def af_copy(p, g):
        return remote(
            maps[p].at[g, :, pl.ds(0, hwidth)], sibs[p].at[g], af_s.at[p, g], af_r.at[p, g], "mlp", sib
        )

    def share(p, g):
        if p in sibs:
            af_copy(p, g).start()

    def tok_sib(k, who):
        return remote(
            tokens_ref.at[rows_of(k)], whole.at[who, rows_of(k)], ts_s.at[k], ts_r.at[k], "mlp", sib
        )

    def tok_far(k, who):
        return remote(
            tokens_ref.at[rows_of(k)], whole.at[who, rows_of(k)], tc_s.at[k], tc_r.at[k], "mlp", far
        )

    def tok_fwd(k, who):
        return remote(
            whole.at[far, rows_of(k)], whole.at[who, rows_of(k)], tf_s.at[k], tf_r.at[k], "mlp", sib
        )

    def part_sib(k, h):
        return remote(sib_out.at[k, h], sib_in.at[k, h], rs_s.at[h, k], rs_r.at[h, k], "mlp", sib)

    def part_far(k):
        return remote(far_out.at[k], far_in.at[k], rc_s.at[k], rc_r.at[k], "mlp", far)

    tables = [
        local(4, lengths_hbm, lengths_ref),
        local(5, slot_hbm, slot_ref),
        local(6, chosen_hbm, chosen_ref),
        local(7, gain_hbm, gain_ref),
    ]
    load_own = local(3, tokens_ref, whole.at[m])
    load_gate = local(0, gate_ref, gu_v.at[:, pl.ds(0, inner)])
    load_up = local(1, up_ref, gu_v.at[:, pl.ds(inner, inner)])
    load_down = local(2, down_ref, down_v.at[pl.ds(0, inner)])
    mine = pl.ds(pl.multiple_of(half * hwidth, hwidth), hwidth)
    other = pl.ds(pl.multiple_of((1 - half) * hwidth, hwidth), hwidth)
    left, right = pl.ds(0, hwidth), pl.ds(hwidth, inner)
    packs = []
    for o in range(owned):
        two, one = pl.ds(o * 2 * rank, 2 * rank), pl.ds(o * rank, rank)
        packs += [
            (a_ref.at[o, :, mine], maps_a.at[r, two]),
            (b_ref.at[o], maps_b.at[r, two]),
            (da_ref.at[o], maps_d.at[r, one, right]),
            (db_ref.at[o, :, mine], maps_d.at[r, one, left]),
        ]
    packs = [local(8 + i, src, dst) for i, (src, dst) in enumerate(packs)]

    barrier = pltpu.get_barrier_semaphore()

    def greet(axis, dev):
        pl.semaphore_signal(barrier, inc=1, device_id={axis: dev}, device_id_type=MESH)

    greet("mlp", sib)
    greet("mlp", far)
    greet("req", partner)
    inner_up = place < places - 1
    inner_down = place > 0
    @pl.when(inner_up)
    def _():
        greet("req", r + 2)

    @pl.when(inner_down)
    def _():
        greet("req", r - 2)

    for copy in packs:
        copy.start()
    below = (place + places - 1) // places
    above = (2 * (places - 1) - place) // places
    pl.semaphore_wait(barrier, 3 + below + above)

    def each(n, start=0):
        def deco(f):
            def body(i, carry):
                f(i)
                return carry

            lax.fori_loop(start, n, body, 0)

        return deco

    @each(CHUNKS)
    def _(k):
        tok_far(k, m).start()
        tok_sib(k, m).start()

    for copy in packs:
        copy.wait()

    def send_own(p):
        @pl.when(inner_up)
        def _():
            up_copy(p, place).start()

        @pl.when(inner_down)
        def _():
            down_copy(p, place).start()

        cross_copy(p, place, lane).start()
        share(p, r)

    for p in PIECES:
        send_own(p)
    for copy in [load_own, load_gate, load_up, load_down] + tables:
        copy.start()

    def relay(p, part):
        def body(d, carry):
            @pl.when(place - d >= 0)
            def _():
                i = place - d
                up_copy(p, i).wait_recv()

                @pl.when(inner_up)
                def _():
                    up_copy(p, i).start()

                cross_copy(p, i, lane).start()
                share(p, 2 * i + lane)

            @pl.when(place + d < places)
            def _():
                i = place + d
                down_copy(p, i).wait_recv()

                @pl.when(inner_down)
                def _():
                    down_copy(p, i).start()

                cross_copy(p, i, lane).start()
                share(p, 2 * i + lane)

            return carry

        first = 1 + (places - 1) * part // 3
        last = 1 + (places - 1) * (part + 1) // 3
        lax.fori_loop(first, last, body, 0)

    def crossed(p):
        @each(places)
        def _(i):
            cross_copy(p, i, 1 - lane).wait_recv()
            share(p, 2 * i + 1 - lane)

    def gathered(p):
        @each(groups)
        def _(g):
            af_copy(p, g).wait_recv()

    def pick(q):
        chosen = chosen_ref[slot_ref[q, r]]
        if owned > 1:
            return chosen // owned, lax.rem(chosen, owned)
        return chosen, 0

    def take_ab():
        crossed_cols = ((mine, maps_a), (other, sib_a))
        for q in range(slots):
            g, o = pick(q)
            one, two = pl.ds(o * 2 * rank, rank), pl.ds(o * 2 * rank + rank, rank)
            at, at2 = pl.ds(q * rank, rank), pl.ds(span + q * rank, rank)
            for dst, part in crossed_cols:
                a_sel[at, dst] = part[g, one, :]
                a_sel[at2, dst] = part[g, two, :]
            bg_sel[at, :] = maps_b[g, one, :]
            bu_sel[at2, :] = maps_b[g, two, :]

    def take_d():
        for q in range(slots):
            g, o = pick(q)
            one = pl.ds(o * rank, rank)
            at, at2 = pl.ds(q * rank, rank), pl.ds(span + q * rank, rank)
            for dst, part in ((mine, maps_d), (other, sib_d)):
                db = part[g, one, 0:hwidth]
                down_v[pl.ds(inner + q * rank, rank), dst] = db
                down_v[pl.ds(inner + span + q * rank, rank), dst] = db
            da = maps_d[g, one, hwidth : hwidth + inner]
            da_sel[at, :] = da
            da_sel[at2, :] = da

    def live_rows(k):
        column = lax.broadcasted_iota(jnp.int32, (1, 2 * span), 1)
        column = jnp.where(column < span, column, column - span)
        low = jnp.zeros((1, 2 * span), jnp.int32)
        high = jnp.zeros((1, 2 * span), jnp.int32)
        end = 0
        for q in range(slots):
            own_q = (column >= q * rank) & (column < (q + 1) * rank)
            low = jnp.where(own_q, end, low)
            end = end + lengths_ref[q, r]
            high = jnp.where(own_q, end, high)
        at = lax.broadcasted_iota(jnp.int32, (rc, 2 * span), 0) + k * rc
        return (at >= low) & (at < high)

    def pass_on(k):
        tok_far(k, far).wait_recv()
        tok_fwd(k, far).start()

    def norm(k):
        here = rows_of(k)
        tok_sib(k, sib).wait_recv()
        tok_fwd(k, diag).wait_recv()
        gain_row = gain_ref[...].astype(f32).reshape(1, -1)
        squares = jnp.zeros((rc, 1), f32)
        for b in range(parts):
            x = whole[b, here, :].astype(f32)
            squares += jnp.sum(x * x, axis=1, keepdims=True)
        scale = lax.rsqrt(squares / width + EPSILON)
        for b in range(parts):
            x = whole[b, here, :].astype(f32)
            gain = gain_row[:, b * cols : (b + 1) * cols]
            normed[k, :, b * cols : (b + 1) * cols] = (x * scale * gain).astype(bf16)

    tiles = list(range(0, 2 * inner, 256))

    def base(k, first, last):
        for n0 in tiles[first:last]:
            n1 = min(n0 + 256, 2 * inner)
            gu_sum[k, :, n0:n1] = jnp.dot(normed[k], gu_v[:, n0:n1], preferred_element_type=f32)

    def gated(k):
        live = live_rows(k)
        low_rank = lax.dot_general(normed[k], a_sel[...], NT, preferred_element_type=f32)
        low_rank = jnp.where(live, low_rank, 0.0).astype(bf16)
        for n0 in range(0, inner, 256):
            n1 = min(n0 + 256, inner)
            g = gu_sum[k, :, n0:n1]
            g += jnp.dot(low_rank, bg_sel[:, n0:n1], preferred_element_type=f32)
            u = gu_sum[k, :, inner + n0 : inner + n1]
            u += jnp.dot(low_rank, bu_sel[:, n0:n1], preferred_element_type=f32)
            hidden[:, n0:n1] = (jax.nn.silu(g) * u).astype(bf16)

    def projected(k):
        live = live_rows(k)
        down_rank = lax.dot_general(hidden[:, :inner], da_sel[...], NT, preferred_element_type=f32)
        down_rank = jnp.where(live, down_rank, 0.0)
        coarse = down_rank.astype(bf16).astype(f32)
        column = lax.broadcasted_iota(jnp.int32, (rc, 2 * span), 1)
        down_rank = jnp.where(column < span, coarse, down_rank - coarse).astype(bf16)
        hidden[:, inner:] = down_rank

        def part_of(b):
            there = pl.ds(pl.multiple_of(b * cols, cols), cols)
            return jnp.dot(hidden[...], down_v[:, there], preferred_element_type=f32)

        sib_out[k, 0] = part_of(diag).astype(bf16)
        part_sib(k, 0).start()
        sib_out[k, 1] = part_of(sib).astype(bf16)
        part_sib(k, 1).start()
        own_part[k, 0] = part_of(far)
        own_part[k, 1] = part_of(m)

    def reduce_far(k):
        part_sib(k, 0).wait_recv()
        far_out[k] = (own_part[k, 0] + sib_in[k, 0].astype(f32)).astype(bf16)
        part_far(k).start()

    for p in PIECES:
        relay(p, 0)
    relay(A, 1)
    bg_sel[...] = jnp.zeros_like(bg_sel)
    bu_sel[...] = jnp.zeros_like(bu_sel)
    for copy in [load_own, load_gate, load_up] + tables:
        copy.wait()

    @each(CHUNKS + 2)
    def _(j):
        def at(step):
            return pl.when(j == step)

        has_base = (j < 2) | (j == 3) | (j == 4)
        has_rest = j >= 2
        kb = jnp.where(j < 2, j, j - 1)
        kr = j - 2

        @at(1)
        def _():
            relay(D, 2)

        @pl.when(j < 2)
        def _():
            pass_on(j)

        @at(0)
        def _():
            relay(D, 1)

        @at(1)
        def _():
            relay(B, 2)

        @pl.when(has_base)
        def _():
            norm(kb)

        @pl.when(has_base)
        def _():
            base(kb, 0, 3)

        @pl.when(has_base & has_rest)
        def _():
            reduce_far(j - 3)

        @at(0)
        def _():
            relay(B, 1)

        @pl.when(has_base)
        def _():
            base(kb, 3, len(tiles))

        @at(0)
        def _():
            relay(A, 2)

        @at(2)
        def _():
            crossed(A)
            crossed(D)
            crossed(B)
            gathered(A)
            take_ab()

        @pl.when(has_rest)
        def _():
            gated(kr)

        @at(2)
        def _():
            pass_on(2)
            gathered(D)
            load_down.wait()
            take_d()

        @at(3)
        def _():
            pass_on(3)

        @at(5)
        def _():
            reduce_far(2)

        @pl.when(has_rest)
        def _():
            projected(kr)

    reduce_far(3)

    total = 0
    for q in range(slots):
        total = total + lengths_ref[q, r]

    @each(CHUNKS)
    def _(k):
        here = rows_of(k)
        part_sib(k, 1).wait_recv()
        part_far(k).wait_recv()
        branch = own_part[k, 1] + sib_in[k, 1].astype(f32) + far_in[k].astype(f32)
        branch = branch.astype(bf16).astype(f32)
        at = lax.broadcasted_iota(jnp.int32, (rc, cols), 0) + k * rc
        x = whole[m, here, :].astype(f32)
        out_ref[here, :] = jnp.where(at < total, x + branch, x).astype(out_ref.dtype)

    @each(CHUNKS)
    def _(k):
        tok_far(k, m).wait_send()
        tok_sib(k, m).wait_send()
        tok_fwd(k, far).wait_send()
        part_sib(k, 0).wait_send()
        part_sib(k, 1).wait_send()
        part_far(k).wait_send()

    for p in PIECES:

        @each(places)
        def _(i):
            cross_copy(p, i, lane).wait_send()

            @pl.when(inner_up & (i <= place))
            def _():
                up_copy(p, i).wait_send()

            @pl.when(inner_down & (i >= place))
            def _():
                down_copy(p, i).wait_send()

        if p in sibs:

            @each(groups)
            def _(g):
                af_copy(p, g).wait_send()


def on_device(
    tokens,
    norm_gain_vector,
    gate_weight,
    up_weight,
    down_weight,
    gate_up_input_maps,
    gate_up_output_maps,
    down_input_maps,
    down_output_maps,
    lengths,
    request_adapter_slot,
    selected,
):
    groups = lax.axis_size("req")
    parts = lax.axis_size("mlp")
    rows, cols = tokens.shape
    owned, rank, width = down_output_maps.shape
    inner = gate_weight.shape[1]
    slots = lengths.shape[1]
    span = slots * rank
    hwidth = width // 2
    bf16, f32 = jnp.bfloat16, jnp.float32

    rc = rows // CHUNKS
    vm, hbm = (pl.BlockSpec(memory_space=s) for s in (pltpu.VMEM, pl.ANY))
    dma = pltpu.SemaphoreType.DMA
    buffers = [
        pltpu.SMEM((slots, groups), jnp.int32),
        pltpu.SMEM((slots, groups), jnp.int32),
        pltpu.SMEM(selected.shape, jnp.int32),
        pltpu.VMEM(norm_gain_vector.shape, bf16),
        pltpu.VMEM((width, 2 * inner), bf16),
        pltpu.VMEM((inner + 2 * span, width), bf16),
        pltpu.VMEM((parts, rows, cols), bf16),
        pltpu.VMEM((CHUNKS, rc, width), bf16),
        pltpu.VMEM((CHUNKS, rc, 2 * inner), f32),
        pltpu.VMEM((rc, inner + 2 * span), bf16),
        pltpu.VMEM((groups, owned * 2 * rank, hwidth), bf16),
        pltpu.VMEM((groups, owned * 2 * rank, inner), bf16),
        pltpu.VMEM((groups, owned * rank, hwidth + inner), bf16),
        pltpu.VMEM((groups, owned * 2 * rank, hwidth), bf16),
        pltpu.VMEM((groups, owned * rank, hwidth), bf16),
        pltpu.VMEM((2 * span, width), bf16),
        pltpu.VMEM((2 * span, inner), bf16),
        pltpu.VMEM((2 * span, inner), bf16),
        pltpu.VMEM((2 * span, inner), bf16),
        pltpu.VMEM((CHUNKS, 2, rc, cols), f32),
        pltpu.VMEM((CHUNKS, 2, rc, cols), bf16),
        pltpu.VMEM((CHUNKS, 2, rc, cols), bf16),
        pltpu.VMEM((CHUNKS, rc, cols), bf16),
        pltpu.VMEM((CHUNKS, rc, cols), bf16),
    ]
    held = sum(math.prod(b.shape) * jnp.dtype(b.dtype).itemsize for b in buffers)
    return pl.pallas_call(
        functools.partial(kernel, groups, owned, rank, slots),
        out_shape=jax.ShapeDtypeStruct((rows, cols), tokens.dtype),
        in_specs=[hbm] * 12,
        out_specs=vm,
        scratch_shapes=buffers
        + [dma((3, groups // 2)) for _ in range(5)]
        + [dma((3, groups)) for _ in range(2)]
        + [dma((CHUNKS,)) for _ in range(6)]
        + [dma((2, CHUNKS)) for _ in range(2)]
        + [dma((CHUNKS,)) for _ in range(2)]
        + [dma((8 + 4 * owned,))],
        compiler_params=pltpu.CompilerParams(
            collective_id=0, has_side_effects=True, vmem_limit_bytes=min(held + 6 * 1024 * 1024, 60 * 1024 * 1024)
        ),
    )(
        *(
            pltpu.with_memory_space_constraint(x, pltpu.HBM)
            for x in (
                lengths.T,
                request_adapter_slot.T,
                selected,
                tokens,
                norm_gain_vector,
                gate_weight,
                up_weight,
                down_weight,
                jnp.swapaxes(gate_up_input_maps, 1, 2),
                gate_up_output_maps.reshape(owned, 2 * rank, inner),
                jnp.swapaxes(down_input_maps, 1, 2),
                down_output_maps,
            )
        ),
    )


def solution(mesh):
    in_specs = (
        P("req", "mlp"),
        P(),
        P(None, "mlp"),
        P(None, "mlp"),
        P("mlp", None),
        P("req", None, None),
        P("req", None, None, "mlp"),
        P("req", "mlp", None),
        P("req", None, None),
        P(),
        P(),
        P(),
    )
    return jax.shard_map(
        on_device, mesh=mesh, in_specs=in_specs, out_specs=P("req", "mlp"), check_vma=False
    )
```
